256 devices in a mesh: blk: 16 (over x_hi, z), wide: 16 (over y, x_lo, core).
Axes of the slice: x: 4 (x_hi: 2, x_lo: 2; x = x_hi * 2 + x_lo), y: 4, z: 8, core: 2. Of those that a mesh axis runs over, the one named last changes fastest.
Arguments:
- blocks: bfloat16 [4096, 64, 4096], P(('blk', 'wide')), may hold values from -24 to 24
- block_row: int32 [4096], P(('blk', 'wide')), may hold values from 0 to 3
- block_depth: int32 [4096], P(('blk', 'wide')), may hold values from 0 to 15
- live: int32 [4096], P(('blk', 'wide')), may hold values from 0 to 1, as said below
- factor_b: bfloat16 [1024, 256], P('blk'), may hold values from -6 to 6
- factor_c: bfloat16 [1024, 256], replicated, may hold values from -6 to 6
Outputs:
- factor_a: bfloat16 [4096, 256], P('wide')
- factor_b_new: bfloat16 [1024, 256], P(('blk', 'wide'))
The draws below stay inside these ranges and needn't reach their ends.
Inputs may be any that keep to these rules, and one draw needn't show every extreme that they name: 1 marks a slot that holds a block, 0 an empty one; the share of live slots differs between devices, and slots 0 to 15 are all live.
All inputs are finite; a program needn't handle non-finite values.
Results may differ from the reference program's by a relative error of at most 0.0091.
Values may be sent and summed in bfloat16 or wider, within the bound.
A program may use at most 64 MiB of HBM per device.

```python
import math
import jax
import jax.numpy as jnp
from jax import lax

RANK = 256
BLOCK = 64
ROW_BLOCKS = 4
DEPTH_BLOCKS = 16
SLOT_COUNT = 16
SLICES = 16
SLICE_ROWS = 256
ROWS_A = 4096
ROWS_B = 1024
ROWS_C = 1024
SLOTS = 4096


def draw_live(key, part):
    owners_count = SLOTS // SLOT_COUNT
    rates = jax.random.randint(jax.random.fold_in(key, 11), (owners_count,), 1, SLOT_COUNT + 1)
    rates = rates.at[0].set(SLOT_COUNT)
    picks = jax.random.randint(jax.random.fold_in(key, 12), (SLOTS,), 0, SLOT_COUNT)
    owner = jnp.arange(SLOTS, dtype=jnp.int32) // SLOT_COUNT
    return (picks < rates[owner]).astype(jnp.int32)


def mixed_columns(random_part, decay_rate):
    mixed_sum = random_part[:, 15:15 + RANK]
    energy = 1.0
    for lag_index in range(1, 16):
        weight_now = decay_rate ** lag_index
        start_col = 15 - lag_index
        mixed_sum = mixed_sum + weight_now * random_part[:, start_col:start_col + RANK]
        energy = energy + weight_now * weight_now
    return mixed_sum / math.sqrt(energy)


def drawn_factor(key, row_count, salt):
    random_part = jax.random.normal(jax.random.fold_in(key, salt), (row_count, RANK + 15), jnp.float32)
    values = mixed_columns(random_part, 0.9)
    return jnp.clip(values, -6.0, 6.0)


def draw_factor_b(key, part):
    values = drawn_factor(key, ROWS_B, 23)
    return values.astype(jnp.bfloat16)


def draw_factor_c(key, part):
    values = drawn_factor(key, ROWS_C, 33)
    return values.astype(jnp.bfloat16)


def set_ends(array, rng, low, top_value):
    extent = array.shape
    spot = [jax.random.randint(jax.random.fold_in(rng, axis), (), 0, extent[axis]) for axis in range(len(extent))]
    array = array.at[tuple(spot)].set(low)
    longest = extent.index(max(extent))
    spot[longest] = (spot[longest] + 1) % extent[longest]
    return array.at[tuple(spot)].set(top_value)


def strengthened(entries, own_key, source, target, shards_of, factor):
    owner, partner = [(jnp.arange(entries.shape[dim]) // (entries.shape[dim] // shards_of)).reshape([-1 if axis == dim else 1 for axis in range(entries.ndim)]) for dim in (source, target)]
    chosen = jax.random.permutation(own_key, shards_of)[partner]
    strong = (owner == chosen) | (owner == (partner + shards_of // 2) % shards_of)
    return jnp.where(strong, factor * entries, entries)


def block_scale(stream_key, dims, split, least, top_value):
    def one(position, parts):
        draws = jax.random.uniform(jax.random.fold_in(jax.random.fold_in(stream_key, 6), position), (parts,), jnp.float32, least / len(split), top_value / len(split))
        return jnp.repeat(jnp.exp(draws), dims[position] // parts).reshape((-1,) + (1,) * (len(dims) - position - 1))

    gain = one(*split[0])
    for cut in split[1:]:
        gain = gain * one(*cut)
    return gain


def bell_draw_with(key, dims, deviation, bound, shards, heavy, kind=jnp.bfloat16):
    result = deviation * jax.random.normal(key, dims, jnp.float32)
    if shards:
        result = result * block_scale(key, dims, shards, -0.22, 0.18)
    return jnp.clip(strengthened(result, jax.random.fold_in(key, 3), *heavy), -bound, bound).astype(kind)


def setup_inputs(seed: int = 0) -> dict:
    seeds = jax.random.split(jax.random.key(seed), 7)
    blocks = bell_draw_with(seeds[0], (SLOTS, BLOCK, BLOCK * BLOCK), 1.0, 24.0, ((0, 256),), (0, 2, 256, 6.0))
    block_row = set_ends(jax.random.randint(seeds[1], (SLOTS,), 0, ROW_BLOCKS), jax.random.fold_in(seeds[1], 1), 0, ROW_BLOCKS - 1).astype(jnp.int32)
    block_depth = set_ends(jax.random.randint(seeds[2], (SLOTS,), 0, DEPTH_BLOCKS), jax.random.fold_in(seeds[2], 1), 0, DEPTH_BLOCKS - 1).astype(jnp.int32)
    live = draw_live(jax.random.fold_in(seeds[6], 71), 0)
    factor_b = draw_factor_b(jax.random.fold_in(seeds[6], 71), 0)
    factor_c = draw_factor_c(jax.random.fold_in(seeds[6], 71), 0)
    return dict(blocks=blocks, block_row=block_row, block_depth=block_depth, live=live, factor_b=factor_b, factor_c=factor_c)


RIDGE = 0.05

def factor_solve(partial_rows, gram):
    size = gram.shape[0]
    system = gram + RIDGE * jnp.eye(size, dtype=jnp.float32)
    lower = jnp.linalg.cholesky(system)
    solved = jax.scipy.linalg.cho_solve((lower, True), partial_rows.T)
    return solved.T * (0.125 / BLOCK)

def first_term(block, brows, crows):
    width = brows.shape[1]
    paired = (brows.astype(jnp.float32)[:, None, :] * crows.astype(jnp.float32)[None, :, :]).astype(jnp.bfloat16)
    return jnp.dot(block.astype(jnp.float32), paired.reshape(-1, width).astype(jnp.float32), preferred_element_type=jnp.float32)

def second_term(block, arows, crows):
    edge = arows.shape[0]
    paired = (arows.astype(jnp.float32)[:, None, :] * crows.astype(jnp.float32)[None, :, :]).astype(jnp.bfloat16)
    cube = block.reshape(edge, edge, edge)
    return lax.dot_general(cube.astype(jnp.float32), paired.astype(jnp.float32), (((0, 2), (0, 1)), ((), ())), preferred_element_type=jnp.float32)

def reference(blocks, block_row, block_depth, live, factor_b, factor_c):
    edge = BLOCK
    weights = live.astype(jnp.float32)
    gram_c = jnp.dot(factor_c.T.astype(jnp.float32), factor_c.astype(jnp.float32), preferred_element_type=jnp.float32) / ROWS_C
    gram_b = jnp.dot(factor_b.T.astype(jnp.float32), factor_b.astype(jnp.float32), preferred_element_type=jnp.float32) / ROWS_B

    def place(index):
        slot = index.astype(jnp.int32)
        group = slot % SLOT_COUNT
        slice_index = slot // SLOT_COUNT % SLICES
        first_row = (slice_index * SLICE_ROWS + block_row[slot] * edge).astype(jnp.int32)
        depth_row = (block_depth[slot] * edge).astype(jnp.int32)
        return (slot, (group * edge).astype(jnp.int32), first_row, depth_row)

    def first_loop(index, total):
        slot, panel_row, first_row, depth_row = place(index)
        brows = lax.dynamic_slice_in_dim(factor_b, panel_row, edge, 0)
        crows = lax.dynamic_slice_in_dim(factor_c, depth_row, edge, 0)
        term = first_term(blocks[slot], brows, crows) * weights[slot]
        current = lax.dynamic_slice_in_dim(total, first_row, edge, 0)
        return lax.dynamic_update_slice_in_dim(total, current + term, first_row, 0)
    mttkrp_a = lax.fori_loop(0, SLOTS, first_loop, jnp.zeros((ROWS_A, RANK), jnp.float32))
    factor_a = factor_solve(mttkrp_a, gram_c * gram_b).astype(jnp.bfloat16)
    gram_a = jnp.dot(factor_a.T.astype(jnp.float32), factor_a.astype(jnp.float32), preferred_element_type=jnp.float32) / ROWS_A

    def second_loop(index, total):
        slot, panel_row, first_row, depth_row = place(index)
        arows = lax.dynamic_slice_in_dim(factor_a, first_row, edge, 0)
        crows = lax.dynamic_slice_in_dim(factor_c, depth_row, edge, 0)
        term = second_term(blocks[slot], arows, crows) * weights[slot]
        current = lax.dynamic_slice_in_dim(total, panel_row, edge, 0)
        return lax.dynamic_update_slice_in_dim(total, current + term, panel_row, 0)
    mttkrp_b = lax.fori_loop(0, SLOTS, second_loop, jnp.zeros((ROWS_B, RANK), jnp.float32))
    factor_b_new = factor_solve(mttkrp_b, gram_c * gram_a).astype(jnp.bfloat16)
    return (factor_a, factor_b_new)
```

```python
import functools

import jax
import jax.numpy as jnp
from jax import lax
from jax.experimental import pallas as pl
from jax.experimental.pallas import tpu as pltpu
from jax.sharding import PartitionSpec as P

EDGE = 64
RANK = 256
ROW_BLOCKS = 4
RIDGE = 0.05
SCALE = 0.125 / EDGE
PANEL = 32
F32 = jnp.float32
BF16 = jnp.bfloat16
MESH = pl.DeviceIdType.MESH
TN = (((0,), (0,)), ((), ()))


def split3(x):
    hi = x.astype(BF16)
    rest = x - hi.astype(F32)
    mid = rest.astype(BF16)
    low = (rest - mid.astype(F32)).astype(BF16)
    return hi, mid, low


def small_inverse(cols):
    sub = lax.broadcasted_iota(jnp.int32, (8, 128), 0)
    for k in range(8):
        row = [c[k : k + 1, :] for c in cols]
        inv = 1.0 / jnp.broadcast_to(row[k], (8, 128))
        here = sub == k
        pivot_col = cols[k]
        new = []
        for j in range(8):
            if j == k:
                new.append(jnp.where(here, inv, -pivot_col * inv))
            else:
                scaled = row[j] * inv
                new.append(jnp.where(here, scaled, cols[j] - pivot_col * scaled))
        cols = new
    return cols


def panel_eliminate(groups):
    lane = lax.broadcasted_iota(jnp.int32, (8, RANK), 1)
    count = len(groups)
    for s in range(count):
        base = 8 * s
        cols = [
            jnp.broadcast_to(groups[s][:, base + j : base + j + 1], (8, 128)) for j in range(8)
        ]
        others = {
            g: [jnp.broadcast_to(groups[g][:, base + j : base + j + 1], (8, RANK)) for j in range(8)]
            for g in range(count)
            if g != s
        }
        inv = [jnp.concatenate([c, c], axis=1) for c in small_inverse(cols)]
        terms = [inv[j] * groups[s][j : j + 1, :] for j in range(8)]
        while len(terms) > 1:
            terms = [terms[i] + terms[i + 1] for i in range(0, len(terms), 2)]
        rows = terms[0]
        for j in range(8):
            rows = jnp.where(lane == base + j, inv[j], rows)
        inside = (lane >= base) & (lane < base + 8)
        new = []
        for g in range(count):
            if g == s:
                new.append(rows)
                continue
            kept = jnp.where(inside, 0.0, groups[g])
            parts = [others[g][j] * rows[j : j + 1, :] for j in range(8)]
            while len(parts) > 1:
                parts = [parts[i] + parts[i + 1] for i in range(0, len(parts), 2)]
            new.append(kept - parts[0])
        groups = new
    return groups


def invert_steps(mat, first, last):
    lane = lax.broadcasted_iota(jnp.int32, (1, RANK), 1)

    def step(p, carry):
        r0 = pl.multiple_of(p * PANEL, PANEL)
        panel = mat[pl.ds(r0, PANEL), :]
        rolled = pltpu.roll(panel, lax.rem(RANK - r0, RANK), 1)
        groups = panel_eliminate([rolled[8 * g : 8 * g + 8, :] for g in range(PANEL // 8)])
        rows = pltpu.roll(jnp.concatenate(groups, axis=0), r0, 1)
        before = lane < r0
        inside = (lane >= r0) & (lane < r0 + PANEL)
        sign = jnp.where(before, -1.0, jnp.where(inside, 0.0, 1.0))
        qh, qm, ql = split3(panel * sign)
        wh, wm, wl = split3(rows)
        left = jnp.concatenate([qh, qh, qh, qm, qm, ql], axis=0)
        right = jnp.concatenate([wh, wm, wl, wh, wm, wh], axis=0)
        for half in range(2):
            cut = pl.ds(half * 128, 128)
            update = lax.dot_general(
                left[:, half * 128 : half * 128 + 128], right, TN, preferred_element_type=F32
            )
            mat[cut, :] = jnp.where(inside, 0.0, mat[cut, :]) - update
        mat[pl.ds(r0, PANEL), :] = rows
        return carry

    lax.fori_loop(first, last, step, 0)


def kernel(
    nb,
    nw,
    total_rows,
    block_row,
    block_depth,
    live,
    blocks,
    fb,
    fc,
    out_a,
    out_b,
    x,
    bg,
    acc,
    ra,
    ca,
    fa,
    gram_c,
    mat_a,
    mat_b,
    gl,
    gr,
    gs,
    gfull,
    bd,
    y,
    tf,
    tsend,
    trecv,
    us,
    ur,
    x_sem,
    b_s,
    b_r,
    ra_s,
    ra_r,
    ca_s,
    ca_r,
    g1_s,
    g1_r,
    g2_s,
    g2_r,
    t_s,
    t_r,
    u_s,
    u_r,
):
    b = lax.axis_index("blk")
    w = lax.axis_index("wide")
    slots = nb
    rc = ROW_BLOCKS * EDGE // nb
    gc = RANK // nb
    fr = EDGE // nw
    own = b == w

    def load_x(s):
        return pltpu.make_async_copy(blocks.at[s], x.at[s], x_sem.at[s])

    def start_x(t, carry):
        load_x(lax.rem(b + t, nb)).start()
        return carry

    lax.fori_loop(0, slots, start_x, 0)

    barrier = pltpu.get_barrier_semaphore()

    def signal(i, j):
        pl.semaphore_signal(barrier, inc=1, device_id=(i, j), device_id_type=MESH)

    def greet_blk(d, carry):
        signal(lax.rem(b + d, nb), w)
        return carry

    def greet_wide(d, carry):
        signal(b, lax.rem(w + d, nw))
        return carry

    def greet_cross(v, carry):
        @pl.when(jnp.logical_not(own & (v == w)))
        def _():
            signal(w, v)

        @pl.when(jnp.logical_not(own & (v == b)))
        def _():
            signal(v, b)

        return carry

    lax.fori_loop(1, nb, greet_blk, 0)
    lax.fori_loop(1, nw, greet_wide, 0)
    lax.fori_loop(0, nw, greet_cross, 0)

    @pl.when(own)
    def _():
        pl.semaphore_wait(barrier, nb - 1 + nw - 1 + 2 * (nw - 1))

    @pl.when(jnp.logical_not(own))
    def _():
        pl.semaphore_wait(barrier, nb - 1 + nw - 1 + 2 * nw)

    def send_b(d):
        return pltpu.make_async_remote_copy(
            src_ref=fb,
            dst_ref=bg.at[b],
            send_sem=b_s.at[d],
            recv_sem=b_r.at[b],
            device_id=(lax.rem(b + d, nb), w),
            device_id_type=MESH,
        )

    def recv_b(s):
        return pltpu.make_async_remote_copy(
            src_ref=fb,
            dst_ref=bg.at[s],
            send_sem=b_s.at[0],
            recv_sem=b_r.at[s],
            device_id=(s, w),
            device_id_type=MESH,
        )

    def start_b(d, carry):
        send_b(d).start()
        return carry

    lax.fori_loop(1, nb, start_b, 0)
    bg[b] = fb[...]
    cfull = fc[...].reshape(fc.shape[0] * EDGE, RANK)
    gram_c[...] = lax.dot_general(cfull, cfull, TN, preferred_element_type=F32) * (
        1.0 / cfull.shape[0]
    )
    acc[...] = jnp.zeros_like(acc)
    bd[...] = jnp.zeros_like(bd)

    def share(g, r):
        row = block_row[g].astype(F32)
        return jnp.maximum(0.0, 1.0 - jnp.abs(row - r)) * live[g].astype(F32)

    def first_slot(g):
        crows = fc[block_depth[g]]
        term = jnp.zeros((EDGE, RANK), F32)
        for jg in range(EDGE // 4):
            brows = bg[g, pl.ds(jg * 4 // 16 * 16, 16), :]
            off = jg * 4 % 16
            pair = jnp.concatenate(
                [brows[off + q : off + q + 1, :] * crows for q in range(4)], axis=0
            )
            term += jnp.dot(
                x[g, :, pl.ds(jg * 256, 256)], pair, preferred_element_type=F32
            )
        for r in range(ROW_BLOCKS):
            cut = pl.ds(r * EDGE, EDGE)
            acc[cut, :] = acc[cut, :] + term * share(g, r)

    def first_loop(t, carry):
        g = lax.rem(b + t, nb)
        load_x(g).wait()

        @pl.when(t > 0)
        def _():
            recv_b(g).wait_recv()

        first_slot(g)
        return carry

    lax.fori_loop(0, slots, first_loop, 0)

    def send_ra(d):
        peer = lax.rem(b + d, nb)
        return pltpu.make_async_remote_copy(
            src_ref=acc.at[pl.ds(pl.multiple_of(peer * rc, rc), rc), :],
            dst_ref=ra.at[b],
            send_sem=ra_s.at[d],
            recv_sem=ra_r.at[b],
            device_id=(peer, w),
            device_id_type=MESH,
        )

    def recv_ra(s):
        return pltpu.make_async_remote_copy(
            src_ref=acc.at[pl.ds(0, rc), :],
            dst_ref=ra.at[s],
            send_sem=ra_s.at[0],
            recv_sem=ra_r.at[s],
            device_id=(s, w),
            device_id_type=MESH,
        )

    def start_ra(d, carry):
        send_ra(d).start()
        return carry

    lax.fori_loop(1, nb, start_ra, 0)

    bfull = bg[...].reshape(nb * EDGE, RANK)
    gram_b = lax.dot_general(bfull, bfull, TN, preferred_element_type=F32) * (1.0 / (nb * EDGE))
    eye = lax.broadcasted_iota(jnp.int32, (RANK, RANK), 0) == lax.broadcasted_iota(
        jnp.int32, (RANK, RANK), 1
    )
    mat_a[...] = gram_c[...] * gram_b + jnp.where(eye, RIDGE, 0.0)
    invert_steps(mat_a, 0, RANK // PANEL)

    def sum_ra(d, total):
        s = lax.rem(b + d, nb)
        recv_ra(s).wait_recv()
        return total + ra[s]

    rows_a = lax.fori_loop(1, nb, sum_ra, acc[pl.ds(pl.multiple_of(b * rc, rc), rc), :])
    solved = jnp.dot(
        rows_a, mat_a[...], preferred_element_type=F32, precision=lax.Precision.HIGHEST
    )
    ca[...] = (solved * SCALE).astype(BF16)

    own_rows = pl.ds(pl.multiple_of(b * rc, rc), rc)

    def send_ca(d):
        return pltpu.make_async_remote_copy(
            src_ref=ca,
            dst_ref=fa.at[own_rows, :],
            send_sem=ca_s.at[d],
            recv_sem=ca_r.at[b],
            device_id=(lax.rem(b + d, nb), w),
            device_id_type=MESH,
        )

    def recv_ca(s):
        return pltpu.make_async_remote_copy(
            src_ref=ca,
            dst_ref=fa.at[pl.ds(pl.multiple_of(s * rc, rc), rc), :],
            send_sem=ca_s.at[0],
            recv_sem=ca_r.at[s],
            device_id=(s, w),
            device_id_type=MESH,
        )

    def start_ca(d, carry):
        send_ca(d).start()
        return carry

    def wait_ca(d, carry):
        recv_ca(lax.rem(b + d, nb)).wait_recv()
        return carry

    lax.fori_loop(1, nb, start_ca, 0)
    fa[own_rows, :] = ca[...]
    lax.fori_loop(1, nb, wait_ca, 0)
    out_a[...] = fa[...]

    gl[...] = lax.dot_general(fa[...], fa[...], TN, preferred_element_type=F32)
    own_gram = pl.ds(pl.multiple_of(b * gc, gc), gc)

    def copy_g1(peer, slot, d):
        return pltpu.make_async_remote_copy(
            src_ref=gl.at[own_gram, :],
            dst_ref=gr.at[slot],
            send_sem=g1_s.at[d],
            recv_sem=g1_r.at[slot],
            device_id=(b, peer),
            device_id_type=MESH,
        )

    def start_g1(d, carry):
        copy_g1(lax.rem(w + d, nw), w, d).start()
        return carry

    lax.fori_loop(1, nw, start_g1, 0)

    def copy_t(g, slot):
        return pltpu.make_async_remote_copy(
            src_ref=tsend.at[g],
            dst_ref=trecv.at[slot],
            send_sem=t_s.at[g],
            recv_sem=t_r.at[slot],
            device_id=(b, g),
            device_id_type=MESH,
        )

    def second_slot(g):
        crows = fc[block_depth[g]]
        arows = jnp.zeros((EDGE, RANK), F32)
        for r in range(ROW_BLOCKS):
            arows += fa[pl.ds(r * EDGE, EDGE), :].astype(F32) * share(g, r)
        for q in range(4):
            bd[pl.ds(q * EDGE, EDGE), pl.ds(q * RANK, RANK)] = crows
        lhs = jnp.concatenate(
            [x[g, :, pl.ds(jg * 256, 256)] for jg in range(EDGE // 4)], axis=0
        )
        for q in range(4):
            y[...] = jnp.dot(lhs, bd[:, pl.ds(q * RANK, RANK)], preferred_element_type=F32)
            for jg in range(EDGE // 4):
                prod = y[pl.ds(jg * EDGE, EDGE), :] * arows
                tf[pl.ds(jg * 4 + q, 1), :] = jnp.sum(prod, axis=0, keepdims=True)
        tsend[g] = tf[...].astype(BF16)

    def second_loop(t, carry):
        g = lax.rem(w + 1 + t, nw)
        second_slot(g)

        @pl.when(t < nw - 1)
        def _():
            copy_t(g, w).start()

        return carry

    lax.fori_loop(0, nw // 2, second_loop, 0)

    def sum_g1(d, total):
        s = lax.rem(w + d, nw)
        copy_g1(s, s, 0).wait_recv()
        return total + gr[s]

    gs[...] = lax.fori_loop(1, nw, sum_g1, gl[own_gram, :])

    def copy_g2(peer, rows, slot, d):
        return pltpu.make_async_remote_copy(
            src_ref=gs,
            dst_ref=gfull.at[rows, :],
            send_sem=g2_s.at[d],
            recv_sem=g2_r.at[slot],
            device_id=(peer, w),
            device_id_type=MESH,
        )

    def start_g2(d, carry):
        copy_g2(lax.rem(b + d, nb), own_gram, b, d).start()
        return carry

    lax.fori_loop(1, nb, start_g2, 0)
    gfull[own_gram, :] = gs[...]
    lax.fori_loop(nw // 2, nw, second_loop, 0)

    def wait_g2(d, carry):
        s = lax.rem(b + d, nb)
        copy_g2(s, pl.ds(pl.multiple_of(s * gc, gc), gc), s, 0).wait_recv()
        return carry

    lax.fori_loop(1, nb, wait_g2, 0)
    mat_b[...] = gram_c[...] * (gfull[...] * (1.0 / total_rows)) + jnp.where(eye, RIDGE, 0.0)
    invert_steps(mat_b, 0, RANK // PANEL // 2)

    def sum_t(d, total):
        s = lax.rem(w + d, nw)
        copy_t(s, s).wait_recv()
        return total + trecv[s].astype(F32)

    rows_t = lax.fori_loop(1, nw, sum_t, tf[...])
    for v in range(nw):
        us[v] = rows_t[v * fr : (v + 1) * fr, :]

    def copy_u(v, slot, to_b, to_w):
        return pltpu.make_async_remote_copy(
            src_ref=us.at[v],
            dst_ref=ur.at[slot],
            send_sem=u_s.at[v],
            recv_sem=u_r.at[slot],
            device_id=(to_b, to_w),
            device_id_type=MESH,
        )

    def start_u(v, carry):
        @pl.when(jnp.logical_not(own & (v == w)))
        def _():
            copy_u(v, b, w, v).start()

        return carry

    lax.fori_loop(0, nw, start_u, 0)

    @pl.when(own)
    def _():
        ur[b] = us[w]

    invert_steps(mat_b, RANK // PANEL // 2, RANK // PANEL)

    def sum_u(v, total):
        @pl.when(jnp.logical_not(own & (v == b)))
        def _():
            copy_u(0, v, v, b).wait_recv()

        return total + ur[v]

    rows_b = lax.fori_loop(0, nb, sum_u, jnp.zeros((fr, RANK), F32))
    pad = jnp.concatenate([rows_b] * max(1, 8 // fr), axis=0)
    new_b = jnp.dot(pad, mat_b[...], preferred_element_type=F32, precision=lax.Precision.HIGHEST)
    out_b[...] = (new_b[:fr, :] * SCALE).astype(BF16)

    def drain_blk(d, carry):
        send_b(d).wait_send()
        send_ra(d).wait_send()
        send_ca(d).wait_send()
        copy_g2(lax.rem(b + d, nb), own_gram, b, d).wait_send()
        return carry

    def drain_wide(d, carry):
        peer = lax.rem(w + d, nw)
        copy_g1(peer, w, d).wait_send()
        copy_t(peer, w).wait_send()
        return carry

    def drain_u(v, carry):
        @pl.when(jnp.logical_not(own & (v == w)))
        def _():
            copy_u(v, b, w, v).wait_send()

        return carry

    lax.fori_loop(1, nb, drain_blk, 0)
    lax.fori_loop(1, nw, drain_wide, 0)
    lax.fori_loop(0, nw, drain_u, 0)


def per_device(nb, nw, blocks, block_row, block_depth, live, factor_b, factor_c):
    rows_a = ROW_BLOCKS * EDGE
    rc, gc, fr = rows_a // nb, RANK // nb, EDGE // nw
    vm = pl.BlockSpec(memory_space=pltpu.VMEM)
    sm = pl.BlockSpec(memory_space=pltpu.SMEM)
    dma = pltpu.SemaphoreType.DMA
    return pl.pallas_call(
        functools.partial(kernel, nb, nw, nw * rows_a),
        out_shape=(
            jax.ShapeDtypeStruct((rows_a, RANK), BF16),
            jax.ShapeDtypeStruct((fr, RANK), BF16),
        ),
        in_specs=[sm, sm, sm, pl.BlockSpec(memory_space=pl.ANY), vm, vm],
        out_specs=(vm, vm),
        scratch_shapes=[
            pltpu.VMEM((nb, EDGE, EDGE * EDGE), BF16),
            pltpu.VMEM((nb, EDGE, RANK), BF16),
            pltpu.VMEM((rows_a, RANK), F32),
            pltpu.VMEM((nb, rc, RANK), F32),
            pltpu.VMEM((rc, RANK), BF16),
            pltpu.VMEM((rows_a, RANK), BF16),
            pltpu.VMEM((RANK, RANK), F32),
            pltpu.VMEM((RANK, RANK), F32),
            pltpu.VMEM((RANK, RANK), F32),
            pltpu.VMEM((RANK, RANK), F32),
            pltpu.VMEM((nw, gc, RANK), F32),
            pltpu.VMEM((gc, RANK), F32),
            pltpu.VMEM((RANK, RANK), F32),
            pltpu.VMEM((4 * EDGE, 4 * RANK), BF16),
            pltpu.VMEM((EDGE * EDGE // 4, RANK), F32),
            pltpu.VMEM((EDGE, RANK), F32),
            pltpu.VMEM((nw, EDGE, RANK), BF16),
            pltpu.VMEM((nw, EDGE, RANK), BF16),
            pltpu.VMEM((nw, fr, RANK), F32),
            pltpu.VMEM((nb, fr, RANK), F32),
            dma((nb,)),
            dma((nb,)),
            dma((nb,)),
            dma((nb,)),
            dma((nb,)),
            dma((nb,)),
            dma((nb,)),
            dma((nw,)),
            dma((nw,)),
            dma((nb,)),
            dma((nb,)),
            dma((nw,)),
            dma((nw,)),
            dma((nw,)),
            dma((nb,)),
        ],
        compiler_params=pltpu.CompilerParams(
            collective_id=0, has_side_effects=True, vmem_limit_bytes=60 * 1024 * 1024
        ),
        name="cp_als",
    )(block_row, block_depth, live, blocks, factor_b, factor_c.reshape(-1, EDGE, RANK))


def solution(mesh):
    in_specs = (
        P(("blk", "wide"), None, None),
        P(("blk", "wide")),
        P(("blk", "wide")),
        P(("blk", "wide")),
        P("blk", None),
        P(),
    )
    out_specs = (P("wide", None), P(("blk", "wide"), None))
    body = functools.partial(per_device, mesh.shape["blk"], mesh.shape["wide"])
    return jax.shard_map(
        body, mesh=mesh, in_specs=in_specs, out_specs=out_specs, check_vma=False
    )
```

```python
import functools

import jax
import jax.numpy as jnp
from jax import lax
from jax.experimental import pallas as pl
from jax.experimental.pallas import tpu as pltpu
from jax.sharding import PartitionSpec as P

EDGE = 64
RANK = 256
ROW_BLOCKS = 4
RIDGE = 0.05
SCALE = 0.125 / EDGE
PANEL = 32
F32 = jnp.float32
BF16 = jnp.bfloat16
MESH = pl.DeviceIdType.MESH
TN = (((0,), (0,)), ((), ()))


def split3(x):
    hi = x.astype(BF16)
    rest = x - hi.astype(F32)
    mid = rest.astype(BF16)
    low = (rest - mid.astype(F32)).astype(BF16)
    return hi, mid, low


def small_inverse(cols):
    sub = lax.broadcasted_iota(jnp.int32, (8, 128), 0)
    for k in range(8):
        row = [c[k : k + 1, :] for c in cols]
        inv = 1.0 / jnp.broadcast_to(row[k], (8, 128))
        here = sub == k
        pivot_col = cols[k]
        new = []
        for j in range(8):
            if j == k:
                new.append(jnp.where(here, inv, -pivot_col * inv))
            else:
                scaled = row[j] * inv
                new.append(jnp.where(here, scaled, cols[j] - pivot_col * scaled))
        cols = new
    return cols


def panel_eliminate(groups):
    lane = lax.broadcasted_iota(jnp.int32, (8, RANK), 1)
    count = len(groups)
    for s in range(count):
        base = 8 * s
        cols = [
            jnp.broadcast_to(groups[s][:, base + j : base + j + 1], (8, 128)) for j in range(8)
        ]
        others = {
            g: [jnp.broadcast_to(groups[g][:, base + j : base + j + 1], (8, RANK)) for j in range(8)]
            for g in range(count)
            if g != s
        }
        inv = [jnp.concatenate([c, c], axis=1) for c in small_inverse(cols)]
        terms = [inv[j] * groups[s][j : j + 1, :] for j in range(8)]
        while len(terms) > 1:
            terms = [terms[i] + terms[i + 1] for i in range(0, len(terms), 2)]
        rows = terms[0]
        for j in range(8):
            rows = jnp.where(lane == base + j, inv[j], rows)
        inside = (lane >= base) & (lane < base + 8)
        new = []
        for g in range(count):
            if g == s:
                new.append(rows)
                continue
            kept = jnp.where(inside, 0.0, groups[g])
            parts = [others[g][j] * rows[j : j + 1, :] for j in range(8)]
            while len(parts) > 1:
                parts = [parts[i] + parts[i + 1] for i in range(0, len(parts), 2)]
            new.append(kept - parts[0])
        groups = new
    return groups


def invert_steps(mat, first, last):
    lane = lax.broadcasted_iota(jnp.int32, (1, RANK), 1)

    def step(p, carry):
        r0 = pl.multiple_of(p * PANEL, PANEL)
        panel = mat[pl.ds(r0, PANEL), :]
        rolled = pltpu.roll(panel, lax.rem(RANK - r0, RANK), 1)
        groups = panel_eliminate([rolled[8 * g : 8 * g + 8, :] for g in range(PANEL // 8)])
        rows = pltpu.roll(jnp.concatenate(groups, axis=0), r0, 1)
        before = lane < r0
        inside = (lane >= r0) & (lane < r0 + PANEL)
        sign = jnp.where(before, -1.0, jnp.where(inside, 0.0, 1.0))
        qh, qm, ql = split3(panel * sign)
        wh, wm, wl = split3(rows)
        left = jnp.concatenate([qh, qh, qh, qm, qm, ql], axis=0)
        right = jnp.concatenate([wh, wm, wl, wh, wm, wh], axis=0)
        for half in range(2):
            cut = pl.ds(half * 128, 128)
            update = lax.dot_general(
                left[:, half * 128 : half * 128 + 128], right, TN, preferred_element_type=F32
            )
            mat[cut, :] = jnp.where(inside, 0.0, mat[cut, :]) - update
        mat[pl.ds(r0, PANEL), :] = rows
        return carry

    lax.fori_loop(first, last, step, 0)


def kernel(
    nb,
    nw,
    total_rows,
    block_row_in,
    block_depth_in,
    live_in,
    blocks,
    fb_in,
    fc_in,
    out_a,
    out_b,
    block_row,
    block_depth,
    live,
    fb,
    fc,
    x,
    bg,
    acc,
    ra,
    ca,
    fa,
    gram_c,
    mat_a,
    mat_b,
    gl,
    gr,
    gs,
    gfull,
    bd,
    y,
    tf,
    tsend,
    trecv,
    us,
    ur,
    in_sem,
    x_sem,
    bz_s,
    bz_r,
    bx_s,
    bx_r,
    bc_s,
    bc_r,
    ra_s,
    ra_r,
    ca_s,
    ca_r,
    g1_s,
    g1_r,
    g2_s,
    g2_r,
    t_s,
    t_r,
    u_s,
    u_r,
):
    b = lax.axis_index("blk")
    w = lax.axis_index("wide")
    line = nb // 2
    half = EDGE // 2
    rc = ROW_BLOCKS * EDGE // nb
    gc = RANK // nw
    fr = EDGE // nw
    side = b // line
    place = lax.rem(b, line)
    core = lax.rem(w, 2)
    mate = w + 1 - 2 * core
    flip = w + 2 - 4 * lax.rem(w // 2, 2)
    across = (1 - side) * line + place

    def panel(t):
        k = lax.rem(t, line)
        odd = lax.rem(k, 2)
        d = odd * ((k + 1) // 2) + (1 - odd) * lax.rem(line - k // 2, line)
        return lax.rem(side + t // line, 2) * line + lax.rem(place + d, line)

    barrier = pltpu.get_barrier_semaphore()

    def signal(i, j):
        pl.semaphore_signal(barrier, inc=1, device_id=(i, j), device_id_type=MESH)

    def greet_blk(d, carry):
        signal(lax.rem(b + d, nb), w)
        return carry

    def greet_wide(d, carry):
        signal(b, lax.rem(w + d, nw))
        return carry

    lax.fori_loop(1, nb, greet_blk, 0)
    lax.fori_loop(1, nw, greet_wide, 0)
    signal(across, flip)

    small = [
        pltpu.make_async_copy(src, dst, in_sem.at[i])
        for i, (src, dst) in enumerate(
            [
                (fb_in, fb),
                (fc_in, fc),
                (block_row_in, block_row),
                (block_depth_in, block_depth),
                (live_in, live),
            ]
        )
    ]
    for copy in small:
        copy.start()

    def load_x(s):
        return pltpu.make_async_copy(blocks.at[s], x.at[s], x_sem.at[s])

    def start_x(t, carry):
        load_x(panel(t)).start()
        return carry

    lax.fori_loop(0, nb, start_x, 0)
    for copy in small:
        copy.wait()
    bg[b] = fb[...]
    acc[...] = jnp.zeros_like(acc)
    bd[...] = jnp.zeros_like(bd)
    pl.semaphore_wait(barrier, nb - 1 + nw - 1 + 1)

    rows_mine = pl.ds(pl.multiple_of(core * half, half), half)
    rows_mate = pl.ds(pl.multiple_of((1 - core) * half, half), half)

    def copy_bz(to, p):
        return pltpu.make_async_remote_copy(
            src_ref=fb.at[rows_mine, :],
            dst_ref=bg.at[p, rows_mine, :],
            send_sem=bz_s.at[to],
            recv_sem=bz_r.at[p],
            device_id=(to, w),
            device_id_type=MESH,
        )

    def copy_bx(p):
        return pltpu.make_async_remote_copy(
            src_ref=bg.at[p, rows_mine, :],
            dst_ref=bg.at[p, rows_mine, :],
            send_sem=bx_s.at[p],
            recv_sem=bx_r.at[p],
            device_id=(across, flip),
            device_id_type=MESH,
        )

    def copy_bc(p, rows):
        return pltpu.make_async_remote_copy(
            src_ref=bg.at[p, rows, :],
            dst_ref=bg.at[p, rows, :],
            send_sem=bc_s.at[p],
            recv_sem=bc_r.at[p],
            device_id=(b, mate),
            device_id_type=MESH,
        )

    def copy_own_x():
        return pltpu.make_async_remote_copy(
            src_ref=fb.at[rows_mine, :],
            dst_ref=bg.at[b, rows_mine, :],
            send_sem=bx_s.at[b],
            recv_sem=bx_r.at[b],
            device_id=(across, flip),
            device_id_type=MESH,
        )

    def start_bz(t, carry):
        copy_bz(panel(t), b).start()
        return carry

    lax.fori_loop(1, 2, start_bz, 0)
    copy_own_x().start()
    lax.fori_loop(2, line, start_bz, 0)

    def share(g, r):
        row = block_row[g].astype(F32)
        return jnp.maximum(0.0, 1.0 - jnp.abs(row - r)) * live[g].astype(F32)

    def first_slot(g):
        crows = fc[block_depth[g]]
        term = jnp.zeros((EDGE, RANK), F32)
        for jg in range(EDGE // 4):
            brows = bg[g, pl.ds(jg * 4 // 16 * 16, 16), :]
            off = jg * 4 % 16
            pair = jnp.concatenate(
                [brows[off + q : off + q + 1, :] * crows for q in range(4)], axis=0
            )
            term += jnp.dot(
                x[g, :, pl.ds(jg * 256, 256)], pair, preferred_element_type=F32
            )
        for r in range(ROW_BLOCKS):
            cut = pl.ds(r * EDGE, EDGE)
            acc[cut, :] = acc[cut, :] + term * share(g, r)

    def first_loop(t, carry):
        p = panel(t)

        @pl.when((t > 0) & (t < line))
        def _():
            copy_bz(p, p).wait_recv()
            copy_bx(p).start()
            copy_bc(p, rows_mine).start()

        @pl.when((t >= line) & (t < nb))
        def _():
            copy_bx(p).wait_recv()
            copy_bc(p, rows_mine).start()

        @pl.when(t > 1)
        def _():
            copy_bc(panel(t - 1), rows_mate).wait_recv()

        @pl.when(t > 0)
        def _():
            g = panel(t - 1)
            load_x(g).wait()
            first_slot(g)

        return carry

    cfull = fc[...].reshape(fc.shape[0] * EDGE, RANK)
    gram_c[...] = lax.dot_general(cfull, cfull, TN, preferred_element_type=F32) * (
        1.0 / cfull.shape[0]
    )
    lax.fori_loop(0, nb + 1, first_loop, 0)

    def copy_ra(peer, slot):
        return pltpu.make_async_remote_copy(
            src_ref=acc.at[pl.ds(pl.multiple_of(peer * rc, rc), rc), :],
            dst_ref=ra.at[slot],
            send_sem=ra_s.at[peer],
            recv_sem=ra_r.at[slot],
            device_id=(peer, w),
            device_id_type=MESH,
        )

    def start_ra(t, carry):
        copy_ra(panel(nb - t), b).start()
        return carry

    lax.fori_loop(1, nb, start_ra, 0)

    bfull = bg[...].reshape(nb * EDGE, RANK)
    gram_b = lax.dot_general(bfull, bfull, TN, preferred_element_type=F32) * (1.0 / (nb * EDGE))
    eye = lax.broadcasted_iota(jnp.int32, (RANK, RANK), 0) == lax.broadcasted_iota(
        jnp.int32, (RANK, RANK), 1
    )
    mat_a[...] = gram_c[...] * gram_b + jnp.where(eye, RIDGE, 0.0)
    invert_steps(mat_a, 0, RANK // PANEL)

    own_rows = pl.ds(pl.multiple_of(b * rc, rc), rc)

    def sum_ra(t, total):
        s = panel(t)
        copy_ra(s, s).wait_recv()
        return total + ra[s]

    rows_a = lax.fori_loop(1, nb, sum_ra, acc[own_rows, :])
    solved = jnp.dot(
        rows_a, mat_a[...], preferred_element_type=F32, precision=lax.Precision.HIGHEST
    )
    ca[...] = (solved * SCALE).astype(BF16)

    def copy_ca(peer, s):
        return pltpu.make_async_remote_copy(
            src_ref=ca,
            dst_ref=fa.at[pl.ds(pl.multiple_of(s * rc, rc), rc), :],
            send_sem=ca_s.at[peer],
            recv_sem=ca_r.at[s],
            device_id=(peer, w),
            device_id_type=MESH,
        )

    def start_ca(t, carry):
        copy_ca(panel(nb - t), b).start()
        return carry

    def wait_ca(t, carry):
        s = panel(t)
        copy_ca(s, s).wait_recv()
        return carry

    lax.fori_loop(1, nb, start_ca, 0)
    fa[own_rows, :] = ca[...]
    lax.fori_loop(1, nb, wait_ca, 0)

    gl[...] = lax.dot_general(fa[...], fa[...], TN, preferred_element_type=F32)

    def gram_rows(v):
        return pl.ds(pl.multiple_of(v * gc, gc), gc)

    def copy_g1(peer, slot):
        return pltpu.make_async_remote_copy(
            src_ref=gl.at[gram_rows(peer), :],
            dst_ref=gr.at[slot],
            send_sem=g1_s.at[peer],
            recv_sem=g1_r.at[slot],
            device_id=(b, peer),
            device_id_type=MESH,
        )

    def start_g1(d, carry):
        copy_g1(lax.rem(w + d, nw), w).start()
        return carry

    lax.fori_loop(1, nw, start_g1, 0)
    out_a[...] = fa[...]

    def copy_t(peer, slot):
        return pltpu.make_async_remote_copy(
            src_ref=tsend.at[peer],
            dst_ref=trecv.at[slot],
            send_sem=t_s.at[peer],
            recv_sem=t_r.at[slot],
            device_id=(peer, w),
            device_id_type=MESH,
        )

    def second_slot(g):
        crows = fc[block_depth[g]]
        arows = jnp.zeros((EDGE, RANK), F32)
        for r in range(ROW_BLOCKS):
            arows += fa[pl.ds(r * EDGE, EDGE), :].astype(F32) * share(g, r)
        for q in range(4):
            bd[pl.ds(q * EDGE, EDGE), pl.ds(q * RANK, RANK)] = crows
        lhs = jnp.concatenate(
            [x[g, :, pl.ds(jg * 256, 256)] for jg in range(EDGE // 4)], axis=0
        )
        for q in range(4):
            y[...] = jnp.dot(lhs, bd[:, pl.ds(q * RANK, RANK)], preferred_element_type=F32)
            for jg in range(EDGE // 4):
                prod = y[pl.ds(jg * EDGE, EDGE), :] * arows
                tf[pl.ds(jg * 4 + q, 1), :] = jnp.sum(prod, axis=0, keepdims=True)
        tsend[g] = tf[...].astype(BF16)

    def copy_g2(peer, s):
        return pltpu.make_async_remote_copy(
            src_ref=gs,
            dst_ref=gfull.at[gram_rows(s), :],
            send_sem=g2_s.at[peer],
            recv_sem=g2_r.at[s],
            device_id=(b, peer),
            device_id_type=MESH,
        )

    def second_loop(t, carry):
        g = panel(nb - 1 - t)

        @pl.when(t == nb * 3 // 8)
        def _():
            def sum_g1(d, total):
                s = lax.rem(w + d, nw)
                copy_g1(s, s).wait_recv()
                return total + gr[s]

            def start_g2(d, carry):
                copy_g2(lax.rem(w + d, nw), w).start()
                return carry

            gs[...] = lax.fori_loop(1, nw, sum_g1, gl[gram_rows(w), :])
            lax.fori_loop(1, nw, start_g2, 0)

        second_slot(g)

        @pl.when(t < nb - 1)
        def _():
            copy_t(g, b).start()

        return carry

    lax.fori_loop(0, nb, second_loop, 0)
    gfull[gram_rows(w), :] = gs[...]

    def wait_g2(d, carry):
        s = lax.rem(w + d, nw)
        copy_g2(s, s).wait_recv()
        return carry

    lax.fori_loop(1, nw, wait_g2, 0)
    mat_b[...] = gram_c[...] * (gfull[...] * (1.0 / total_rows)) + jnp.where(eye, RIDGE, 0.0)
    invert_steps(mat_b, 0, RANK // PANEL // 2)

    def sum_t(t, total):
        s = panel(nb - t)
        copy_t(s, s).wait_recv()
        return total + trecv[s].astype(F32)

    rows_t = lax.fori_loop(1, nb, sum_t, tf[...])
    for v in range(nw):
        us[v] = rows_t[v * fr : (v + 1) * fr, :]

    def copy_u(peer, slot):
        return pltpu.make_async_remote_copy(
            src_ref=us.at[peer],
            dst_ref=ur.at[slot],
            send_sem=u_s.at[peer],
            recv_sem=u_r.at[slot],
            device_id=(b, peer),
            device_id_type=MESH,
        )

    def start_u(d, carry):
        copy_u(lax.rem(w + d, nw), w).start()
        return carry

    lax.fori_loop(1, nw, start_u, 0)
    invert_steps(mat_b, RANK // PANEL // 2, RANK // PANEL)

    def sum_u(d, total):
        s = lax.rem(w + d, nw)
        copy_u(s, s).wait_recv()
        return total + ur[s]

    rows_b = lax.fori_loop(1, nw, sum_u, us[w])
    pad = jnp.concatenate([rows_b] * max(1, 8 // fr), axis=0)
    new_b = jnp.dot(pad, mat_b[...], preferred_element_type=F32, precision=lax.Precision.HIGHEST)
    out_b[...] = (new_b[:fr, :] * SCALE).astype(BF16)

    def drain_line(t, carry):
        p = panel(t)
        copy_bz(p, b).wait_send()
        copy_bx(p).wait_send()
        return carry

    def drain_blk(t, carry):
        p = panel(t)
        copy_bc(p, rows_mine).wait_send()
        copy_ra(p, b).wait_send()
        copy_ca(p, b).wait_send()
        copy_t(p, b).wait_send()
        return carry

    def drain_wide(d, carry):
        peer = lax.rem(w + d, nw)
        copy_g1(peer, w).wait_send()
        copy_g2(peer, w).wait_send()
        copy_u(peer, w).wait_send()
        return carry

    copy_own_x().wait_send()
    lax.fori_loop(1, line, drain_line, 0)
    lax.fori_loop(1, nb, drain_blk, 0)
    lax.fori_loop(1, nw, drain_wide, 0)


def per_device(nb, nw, blocks, block_row, block_depth, live, factor_b, factor_c):
    rows_a = ROW_BLOCKS * EDGE
    rc, gc, fr = rows_a // nb, RANK // nw, EDGE // nw
    vm = pl.BlockSpec(memory_space=pltpu.VMEM)
    depth = factor_c.shape[0] // EDGE
    dma = pltpu.SemaphoreType.DMA
    return pl.pallas_call(
        functools.partial(kernel, nb, nw, nw * rows_a),
        out_shape=(
            jax.ShapeDtypeStruct((rows_a, RANK), BF16),
            jax.ShapeDtypeStruct((fr, RANK), BF16),
        ),
        in_specs=[pl.BlockSpec(memory_space=pl.ANY)] * 6,
        out_specs=(vm, vm),
        scratch_shapes=[
            pltpu.SMEM((nb,), jnp.int32),
            pltpu.SMEM((nb,), jnp.int32),
            pltpu.SMEM((nb,), jnp.int32),
            pltpu.VMEM((EDGE, RANK), BF16),
            pltpu.VMEM((depth, EDGE, RANK), BF16),
            pltpu.VMEM((nb, EDGE, EDGE * EDGE), BF16),
            pltpu.VMEM((nb, EDGE, RANK), BF16),
            pltpu.VMEM((rows_a, RANK), F32),
            pltpu.VMEM((nb, rc, RANK), F32),
            pltpu.VMEM((rc, RANK), BF16),
            pltpu.VMEM((rows_a, RANK), BF16),
            pltpu.VMEM((RANK, RANK), F32),
            pltpu.VMEM((RANK, RANK), F32),
            pltpu.VMEM((RANK, RANK), F32),
            pltpu.VMEM((RANK, RANK), F32),
            pltpu.VMEM((nw, gc, RANK), F32),
            pltpu.VMEM((gc, RANK), F32),
            pltpu.VMEM((RANK, RANK), F32),
            pltpu.VMEM((4 * EDGE, 4 * RANK), BF16),
            pltpu.VMEM((EDGE * EDGE // 4, RANK), F32),
            pltpu.VMEM((EDGE, RANK), F32),
            pltpu.VMEM((nb, EDGE, RANK), BF16),
            pltpu.VMEM((nb, EDGE, RANK), BF16),
            pltpu.VMEM((nw, fr, RANK), F32),
            pltpu.VMEM((nw, fr, RANK), F32),
            dma((5,)),
            dma((nb,)),
            dma((nb,)),
            dma((nb,)),
            dma((nb,)),
            dma((nb,)),
            dma((nb,)),
            dma((nb,)),
            dma((nb,)),
            dma((nb,)),
            dma((nb,)),
            dma((nb,)),
            dma((nw,)),
            dma((nw,)),
            dma((nw,)),
            dma((nw,)),
            dma((nb,)),
            dma((nb,)),
            dma((nw,)),
            dma((nw,)),
        ],
        compiler_params=pltpu.CompilerParams(
            collective_id=0, has_side_effects=True, vmem_limit_bytes=60 * 1024 * 1024
        ),
        name="cp_als",
    )(block_row, block_depth, live, blocks, factor_b, factor_c.reshape(-1, EDGE, RANK))


def solution(mesh):
    in_specs = (
        P(("blk", "wide"), None, None),
        P(("blk", "wide")),
        P(("blk", "wide")),
        P(("blk", "wide")),
        P("blk", None),
        P(),
    )
    out_specs = (P("wide", None), P(("blk", "wide"), None))
    body = functools.partial(per_device, mesh.shape["blk"], mesh.shape["wide"])
    return jax.shard_map(
        body, mesh=mesh, in_specs=in_specs, out_specs=out_specs, check_vma=False
    )
```

```python
import functools

import jax
import jax.numpy as jnp
from jax import lax
from jax.experimental import pallas as pl
from jax.experimental.pallas import tpu as pltpu
from jax.sharding import PartitionSpec as P

EDGE = 64
RANK = 256
ROW_BLOCKS = 4
RIDGE = 0.05
SCALE = 0.125 / EDGE
PANEL = 64
LAG = 3
EARLY = 7
F32 = jnp.float32
BF16 = jnp.bfloat16
MESH = pl.DeviceIdType.MESH
TN = (((0,), (0,)), ((), ()))


def split3(x):
    hi = x.astype(BF16)
    rest = x - hi.astype(F32)
    mid = rest.astype(BF16)
    low = (rest - mid.astype(F32)).astype(BF16)
    return hi, mid, low


def small_inverse(cols):
    sub = lax.broadcasted_iota(jnp.int32, (8, 128), 0)
    for k in range(0, 8, 2):
        row0 = [jnp.broadcast_to(c[k : k + 1, :], (8, 128)) for c in cols]
        row1 = [jnp.broadcast_to(c[k + 1 : k + 2, :], (8, 128)) for c in cols]
        p, q, r, s = row0[k], row0[k + 1], row1[k], row1[k + 1]
        inv = 1.0 / (p * s - q * r)
        col0, col1 = cols[k], cols[k + 1]
        new = []
        for j in range(8):
            if j == k:
                up, low = s * inv, -(r * inv)
            elif j == k + 1:
                up, low = -(q * inv), p * inv
            else:
                up = (s * row0[j] - q * row1[j]) * inv
                low = (p * row1[j] - r * row0[j]) * inv
            drop = col0 * up + col1 * low
            rest = -drop if j in (k, k + 1) else cols[j] - drop
            new.append(jnp.where(sub == k, up, jnp.where(sub == k + 1, low, rest)))
        cols = new
    return cols


def panel_eliminate(groups):
    lane = lax.broadcasted_iota(jnp.int32, (8, RANK), 1)
    count = len(groups)
    for s in range(count):
        base = 8 * s
        cols = [
            jnp.broadcast_to(groups[s][:, base + j : base + j + 1], (8, 128)) for j in range(8)
        ]
        others = {
            g: [jnp.broadcast_to(groups[g][:, base + j : base + j + 1], (8, RANK)) for j in range(8)]
            for g in range(count)
            if g != s
        }
        inv = [jnp.concatenate([c, c], axis=1) for c in small_inverse(cols)]
        terms = [inv[j] * groups[s][j : j + 1, :] for j in range(8)]
        while len(terms) > 1:
            terms = [terms[i] + terms[i + 1] for i in range(0, len(terms), 2)]
        rows = terms[0]
        for j in range(8):
            rows = jnp.where(lane == base + j, inv[j], rows)
        inside = (lane >= base) & (lane < base + 8)
        new = []
        for g in range(count):
            if g == s:
                new.append(rows)
                continue
            kept = jnp.where(inside, 0.0, groups[g])
            parts = [others[g][j] * rows[j : j + 1, :] for j in range(8)]
            while len(parts) > 1:
                parts = [parts[i] + parts[i + 1] for i in range(0, len(parts), 2)]
            new.append(kept - parts[0])
        groups = new
    return groups


def invert_steps(mat, first, last):
    lane = lax.broadcasted_iota(jnp.int32, (1, RANK), 1)

    def step(p, carry):
        r0 = pl.multiple_of(p * PANEL, PANEL)
        panel = mat[pl.ds(r0, PANEL), :]
        rolled = pltpu.roll(panel, lax.rem(RANK - r0, RANK), 1)
        groups = panel_eliminate([rolled[8 * g : 8 * g + 8, :] for g in range(PANEL // 8)])
        rows = pltpu.roll(jnp.concatenate(groups, axis=0), r0, 1)
        before = lane < r0
        inside = (lane >= r0) & (lane < r0 + PANEL)
        sign = jnp.where(before, -1.0, jnp.where(inside, 0.0, 1.0))
        qh, qm, ql = split3(panel * sign)
        wh, wm, wl = split3(rows)
        left = jnp.concatenate([qh, qh, qh, qm, qm, ql], axis=0)
        right = jnp.concatenate([wh, wm, wl, wh, wm, wh], axis=0)
        for half in range(2):
            cut = pl.ds(half * 128, 128)
            update = lax.dot_general(
                left[:, half * 128 : half * 128 + 128], right, TN, preferred_element_type=F32
            )
            mat[cut, :] = jnp.where(inside, 0.0, mat[cut, :]) - update
        mat[pl.ds(r0, PANEL), :] = rows
        return carry

    lax.fori_loop(first, last, step, 0)


def kernel(
    nb,
    nw,
    total_rows,
    block_row_in,
    block_depth_in,
    live_in,
    blocks,
    fb_in,
    fc_in,
    out_a,
    out_b,
    block_row,
    block_depth,
    live,
    fb,
    fc,
    x,
    bg,
    acc,
    ra,
    ca,
    fa,
    gram_c,
    mat_a,
    mat_b,
    gl,
    gr,
    gs,
    gfull,
    bd,
    y,
    yc,
    tf,
    tsend,
    trecv,
    us,
    ur,
    cs,
    cr,
    tm,
    in_sem,
    x_sem,
    bz_s,
    bz_r,
    bx_s,
    bx_r,
    bc_s,
    bc_r,
    ra_s,
    ra_r,
    ca_s,
    ca_r,
    g1_s,
    g1_r,
    g2_s,
    g2_r,
    t_s,
    t_r,
    u_s,
    u_r,
    p_s,
    p_r,
):
    b = lax.axis_index("blk")
    w = lax.axis_index("wide")
    line = nb // 2
    half = EDGE // 2
    early = EARLY * nb // 16
    rc = ROW_BLOCKS * EDGE // nb
    gc = RANK // nw
    fr = EDGE // nw
    side = b // line
    place = lax.rem(b, line)
    core = lax.rem(w, 2)
    mate = w + 1 - 2 * core
    flip = w + 2 - 4 * lax.rem(w // 2, 2)
    across = (1 - side) * line + place

    def panel(t):
        k = lax.rem(t, line)
        odd = lax.rem(k, 2)
        d = odd * ((k + 1) // 2) + (1 - odd) * lax.rem(line - k // 2, line)
        return lax.rem(side + t // line, 2) * line + lax.rem(place + d, line)

    def slot_of(t):
        pairs = line // 2
        u = t // 2
        k = lax.rem(u, pairs)
        pair = lax.rem(place // 2 + pairs - 1 - k, pairs)
        far = 1 - u // pairs
        which = lax.rem(t, 2) * core + (1 - lax.rem(t, 2)) * (1 - core)
        return lax.rem(side + far, 2) * line + pair * 2 + which

    barrier = pltpu.get_barrier_semaphore()

    def signal(i, j):
        pl.semaphore_signal(barrier, inc=1, device_id=(i, j), device_id_type=MESH)

    def greet_blk(d, carry):
        signal(lax.rem(b + d, nb), w)
        return carry

    def greet_wide(d, carry):
        signal(b, lax.rem(w + d, nw))
        return carry

    lax.fori_loop(1, nb, greet_blk, 0)
    lax.fori_loop(1, nw, greet_wide, 0)
    signal(across, flip)

    small = [
        pltpu.make_async_copy(src, dst, in_sem.at[i])
        for i, (src, dst) in enumerate(
            [
                (fb_in, fb),
                (fc_in, fc),
                (block_row_in, block_row),
                (block_depth_in, block_depth),
                (live_in, live),
            ]
        )
    ]
    for copy in small:
        copy.start()

    def load_x(s):
        return pltpu.make_async_copy(blocks.at[s], x.at[s], x_sem.at[s])

    def start_x(t, carry):
        load_x(panel(t)).start()
        return carry

    lax.fori_loop(0, nb, start_x, 0)
    for copy in small:
        copy.wait()
    bg[b] = fb[...]
    acc[...] = jnp.zeros_like(acc)
    bd[...] = jnp.zeros_like(bd)
    pl.semaphore_wait(barrier, nb - 1 + nw - 1 + 1)

    rows_mine = pl.ds(pl.multiple_of(core * half, half), half)
    rows_mate = pl.ds(pl.multiple_of((1 - core) * half, half), half)

    def copy_bz(to, p):
        return pltpu.make_async_remote_copy(
            src_ref=fb.at[rows_mine, :],
            dst_ref=bg.at[p, rows_mine, :],
            send_sem=bz_s.at[to],
            recv_sem=bz_r.at[p],
            device_id=(to, w),
            device_id_type=MESH,
        )

    def copy_bx(p):
        return pltpu.make_async_remote_copy(
            src_ref=bg.at[p, rows_mine, :],
            dst_ref=bg.at[p, rows_mine, :],
            send_sem=bx_s.at[p],
            recv_sem=bx_r.at[p],
            device_id=(across, flip),
            device_id_type=MESH,
        )

    def copy_bc(p, rows):
        return pltpu.make_async_remote_copy(
            src_ref=bg.at[p, rows, :],
            dst_ref=bg.at[p, rows, :],
            send_sem=bc_s.at[p],
            recv_sem=bc_r.at[p],
            device_id=(b, mate),
            device_id_type=MESH,
        )

    def copy_own_x():
        return pltpu.make_async_remote_copy(
            src_ref=fb.at[rows_mine, :],
            dst_ref=bg.at[b, rows_mine, :],
            send_sem=bx_s.at[b],
            recv_sem=bx_r.at[b],
            device_id=(across, flip),
            device_id_type=MESH,
        )

    def start_bz(t, carry):
        copy_bz(panel(t), b).start()
        return carry

    lax.fori_loop(1, 2, start_bz, 0)
    copy_own_x().start()
    lax.fori_loop(2, line, start_bz, 0)

    def share(g, r):
        row = block_row[g].astype(F32)
        return jnp.maximum(0.0, 1.0 - jnp.abs(row - r)) * live[g].astype(F32)

    def first_slot(g):
        crows = fc[block_depth[g]]
        term = jnp.zeros((EDGE, RANK), F32)
        for jg in range(EDGE // 4):
            brows = bg[g, pl.ds(jg * 4 // 16 * 16, 16), :]
            off = jg * 4 % 16
            pair = jnp.concatenate(
                [brows[off + q : off + q + 1, :] * crows for q in range(4)], axis=0
            )
            term += jnp.dot(
                x[g, :, pl.ds(jg * 256, 256)], pair, preferred_element_type=F32
            )
        for r in range(ROW_BLOCKS):
            cut = pl.ds(r * EDGE, EDGE)
            acc[cut, :] = acc[cut, :] + term * share(g, r)

    def first_loop(t, carry):
        p = panel(t)

        @pl.when((t > 0) & (t < line))
        def _():
            copy_bz(p, p).wait_recv()
            copy_bx(p).start()
            copy_bc(p, rows_mine).start()

        @pl.when((t >= line) & (t < nb))
        def _():
            copy_bx(p).wait_recv()
            copy_bc(p, rows_mine).start()

        @pl.when(t > LAG)
        def _():
            copy_bc(panel(t - LAG), rows_mate).wait_recv()

        @pl.when(t >= LAG)
        def _():
            g = panel(t - LAG)
            load_x(g).wait()
            first_slot(g)

        return carry

    cfull = fc[...].reshape(fc.shape[0] * EDGE, RANK)
    gram_c[...] = lax.dot_general(cfull, cfull, TN, preferred_element_type=F32) * (
        1.0 / cfull.shape[0]
    )
    lax.fori_loop(1, nb + LAG, first_loop, 0)

    def copy_ra(peer, slot):
        return pltpu.make_async_remote_copy(
            src_ref=acc.at[pl.ds(pl.multiple_of(peer * rc, rc), rc), :],
            dst_ref=ra.at[slot],
            send_sem=ra_s.at[peer],
            recv_sem=ra_r.at[slot],
            device_id=(peer, w),
            device_id_type=MESH,
        )

    def start_ra(t, carry):
        copy_ra(panel(nb - t), b).start()
        return carry

    lax.fori_loop(1, nb, start_ra, 0)

    bfull = bg[...].reshape(nb * EDGE, RANK)
    gram_b = lax.dot_general(bfull, bfull, TN, preferred_element_type=F32) * (1.0 / (nb * EDGE))
    eye = lax.broadcasted_iota(jnp.int32, (RANK, RANK), 0) == lax.broadcasted_iota(
        jnp.int32, (RANK, RANK), 1
    )
    mat_a[...] = gram_c[...] * gram_b + jnp.where(eye, RIDGE, 0.0)
    invert_steps(mat_a, 0, RANK // PANEL)

    own_rows = pl.ds(pl.multiple_of(b * rc, rc), rc)

    def sum_ra(t, total):
        s = panel(t)
        copy_ra(s, s).wait_recv()
        return total + ra[s]

    rows_a = lax.fori_loop(1, nb, sum_ra, acc[own_rows, :])
    solved = jnp.dot(
        rows_a, mat_a[...], preferred_element_type=F32, precision=lax.Precision.HIGHEST
    )
    ca[...] = (solved * SCALE).astype(BF16)

    def copy_ca(peer, s):
        return pltpu.make_async_remote_copy(
            src_ref=ca,
            dst_ref=fa.at[pl.ds(pl.multiple_of(s * rc, rc), rc), :],
            send_sem=ca_s.at[peer],
            recv_sem=ca_r.at[s],
            device_id=(peer, w),
            device_id_type=MESH,
        )

    def start_ca(t, carry):
        copy_ca(panel(nb - t), b).start()
        return carry

    def wait_ca(t, carry):
        s = panel(t)
        copy_ca(s, s).wait_recv()
        return carry

    lax.fori_loop(1, nb, start_ca, 0)
    fa[own_rows, :] = ca[...]

    def depth_operands(g):
        crows = fc[block_depth[g]]
        for q in range(4):
            bd[pl.ds(q * EDGE, EDGE), pl.ds(q * RANK, RANK)] = crows
        return jnp.concatenate(
            [x[g, :, pl.ds(jg * 256, 256)] for jg in range(EDGE // 4)], axis=0
        )

    def early_loop(t, carry):
        lhs = depth_operands(slot_of(t))
        for q in range(4):
            yc[t, q] = jnp.dot(
                lhs, bd[:, pl.ds(q * RANK, RANK)], preferred_element_type=F32
            ).astype(BF16)
        return carry

    lax.fori_loop(0, early, early_loop, 0)
    lax.fori_loop(1, nb, wait_ca, 0)

    gl[...] = lax.dot_general(fa[...], fa[...], TN, preferred_element_type=F32)

    def gram_rows(v):
        return pl.ds(pl.multiple_of(v * gc, gc), gc)

    def copy_g1(peer, slot):
        return pltpu.make_async_remote_copy(
            src_ref=gl.at[gram_rows(peer), :],
            dst_ref=gr.at[slot],
            send_sem=g1_s.at[peer],
            recv_sem=g1_r.at[slot],
            device_id=(b, peer),
            device_id_type=MESH,
        )

    def start_g1(d, carry):
        copy_g1(lax.rem(w + d, nw), w).start()
        return carry

    lax.fori_loop(1, nw, start_g1, 0)
    out_a[...] = fa[...]

    def copy_t(peer, slot):
        return pltpu.make_async_remote_copy(
            src_ref=tsend.at[peer],
            dst_ref=trecv.at[slot],
            send_sem=t_s.at[peer],
            recv_sem=t_r.at[slot],
            device_id=(peer, w),
            device_id_type=MESH,
        )

    def weighted_rows(g):
        arows = jnp.zeros((EDGE, RANK), F32)
        for r in range(ROW_BLOCKS):
            arows += fa[pl.ds(r * EDGE, EDGE), :].astype(F32) * share(g, r)
        return arows

    def second_slot(g):
        arows = weighted_rows(g)
        lhs = depth_operands(g)
        for q in range(4):
            y[...] = jnp.dot(lhs, bd[:, pl.ds(q * RANK, RANK)], preferred_element_type=F32)
            for jg in range(EDGE // 4):
                prod = y[pl.ds(jg * EDGE, EDGE), :] * arows
                tf[pl.ds(jg * 4 + q, 1), :] = jnp.sum(prod, axis=0, keepdims=True)

    def second_early(t, g):
        arows = weighted_rows(g)
        for q in range(4):
            for jg in range(EDGE // 4):
                prod = yc[t, q, pl.ds(jg * EDGE, EDGE), :].astype(F32) * arows
                tf[pl.ds(jg * 4 + q, 1), :] = jnp.sum(prod, axis=0, keepdims=True)

    def copy_g2(peer, s):
        return pltpu.make_async_remote_copy(
            src_ref=gs,
            dst_ref=gfull.at[gram_rows(s), :],
            send_sem=g2_s.at[peer],
            recv_sem=g2_r.at[s],
            device_id=(b, peer),
            device_id_type=MESH,
        )

    def copy_pair(u):
        return pltpu.make_async_remote_copy(
            src_ref=cs.at[u],
            dst_ref=cr.at[u],
            send_sem=p_s.at[u],
            recv_sem=p_r.at[u],
            device_id=(b, mate),
            device_id_type=MESH,
        )

    def pass_on(u):
        copy_pair(u).wait_recv()
        g = slot_of(2 * u + 1)
        tsend[g] = (tm[u] + cr[u]).astype(BF16)

        @pl.when(g != b)
        def _():
            copy_t(g, b).start()

    def after_slot(t):
        u = t // 2

        @pl.when(lax.rem(t, 2) == 0)
        def _():
            cs[u] = tf[...]
            copy_pair(u).start()

        @pl.when(lax.rem(t, 2) == 1)
        def _():
            tm[u] = tf[...]

            @pl.when(u > 0)
            def _():
                pass_on(u - 1)

    def second_first(t, carry):
        second_early(t, slot_of(t))
        after_slot(t)
        return carry

    def second_loop(t, carry):
        @pl.when(t == nb // 2)
        def _():
            def sum_g1(d, total):
                s = lax.rem(w + d, nw)
                copy_g1(s, s).wait_recv()
                return total + gr[s]

            def start_g2(d, carry):
                copy_g2(lax.rem(w + d, nw), w).start()
                return carry

            gs[...] = lax.fori_loop(1, nw, sum_g1, gl[gram_rows(w), :])
            lax.fori_loop(1, nw, start_g2, 0)

        second_slot(slot_of(t))
        after_slot(t)
        return carry

    lax.fori_loop(0, early, second_first, 0)
    lax.fori_loop(early, nb, second_loop, 0)
    pass_on(nb // 2 - 1)
    gfull[gram_rows(w), :] = gs[...]

    def wait_g2(d, carry):
        s = lax.rem(w + d, nw)
        copy_g2(s, s).wait_recv()
        return carry

    lax.fori_loop(1, nw, wait_g2, 0)
    mat_b[...] = gram_c[...] * (gfull[...] * (1.0 / total_rows)) + jnp.where(eye, RIDGE, 0.0)
    invert_steps(mat_b, 0, RANK // PANEL // 2)

    holds = lax.rem(b, 2) == core

    @pl.when(holds)
    def _():
        def sum_t(t, total):
            s = panel(nb - t)
            copy_t(s, s).wait_recv()
            return total + trecv[s].astype(F32)

        own_t = tm[nb // 2 - 1] + cr[nb // 2 - 1]
        rows_t = lax.fori_loop(1, nb, sum_t, own_t)
        for v in range(nw):
            us[v] = rows_t[v * fr : (v + 1) * fr, :]

    def copy_u(peer, slot):
        return pltpu.make_async_remote_copy(
            src_ref=us.at[peer],
            dst_ref=ur.at[slot],
            send_sem=u_s.at[peer],
            recv_sem=u_r.at[slot],
            device_id=(b, peer),
            device_id_type=MESH,
        )

    def start_u(d, carry):
        copy_u(lax.rem(w + d, nw), w).start()
        return carry

    @pl.when(holds)
    def _():
        lax.fori_loop(1, nw, start_u, 0)

    invert_steps(mat_b, RANK // PANEL // 2, RANK // PANEL)

    @pl.when(holds)
    def _():
        ur[w] = us[w]

    def sum_u(i, total):
        s = 2 * i + lax.rem(b, 2)

        @pl.when(s != w)
        def _():
            copy_u(s, s).wait_recv()

        return total + ur[s]

    rows_b = lax.fori_loop(0, nw // 2, sum_u, jnp.zeros((fr, RANK), F32))
    pad = jnp.concatenate([rows_b] * max(1, 8 // fr), axis=0)
    new_b = jnp.dot(pad, mat_b[...], preferred_element_type=F32, precision=lax.Precision.HIGHEST)
    out_b[...] = (new_b[:fr, :] * SCALE).astype(BF16)

    def drain_line(t, carry):
        p = panel(t)
        copy_bz(p, b).wait_send()
        copy_bx(p).wait_send()
        return carry

    def drain_blk(t, carry):
        p = panel(t)
        copy_bc(p, rows_mine).wait_send()
        copy_ra(p, b).wait_send()
        copy_ca(p, b).wait_send()

        @pl.when(lax.rem(p, 2) == core)
        def _():
            copy_t(p, b).wait_send()

        return carry

    def drain_wide(d, carry):
        peer = lax.rem(w + d, nw)
        copy_g1(peer, w).wait_send()
        copy_g2(peer, w).wait_send()

        @pl.when(holds)
        def _():
            copy_u(peer, w).wait_send()

        return carry

    def drain_pair(u, carry):
        copy_pair(u).wait_send()
        return carry

    copy_own_x().wait_send()
    lax.fori_loop(1, line, drain_line, 0)
    lax.fori_loop(1, nb, drain_blk, 0)
    lax.fori_loop(1, nw, drain_wide, 0)
    lax.fori_loop(0, nb // 2, drain_pair, 0)


def per_device(nb, nw, blocks, block_row, block_depth, live, factor_b, factor_c):
    rows_a = ROW_BLOCKS * EDGE
    rc, gc, fr = rows_a // nb, RANK // nw, EDGE // nw
    vm = pl.BlockSpec(memory_space=pltpu.VMEM)
    depth = factor_c.shape[0] // EDGE
    dma = pltpu.SemaphoreType.DMA
    return pl.pallas_call(
        functools.partial(kernel, nb, nw, nw * rows_a),
        out_shape=(
            jax.ShapeDtypeStruct((rows_a, RANK), BF16),
            jax.ShapeDtypeStruct((fr, RANK), BF16),
        ),
        in_specs=[pl.BlockSpec(memory_space=pltpu.HBM)] * 6,
        out_specs=(vm, vm),
        scratch_shapes=[
            pltpu.SMEM((nb,), jnp.int32),
            pltpu.SMEM((nb,), jnp.int32),
            pltpu.SMEM((nb,), jnp.int32),
            pltpu.VMEM((EDGE, RANK), BF16),
            pltpu.VMEM((depth, EDGE, RANK), BF16),
            pltpu.VMEM((nb, EDGE, EDGE * EDGE), BF16),
            pltpu.VMEM((nb, EDGE, RANK), BF16),
            pltpu.VMEM((rows_a, RANK), F32),
            pltpu.VMEM((nb, rc, RANK), F32),
            pltpu.VMEM((rc, RANK), BF16),
            pltpu.VMEM((rows_a, RANK), BF16),
            pltpu.VMEM((RANK, RANK), F32),
            pltpu.VMEM((RANK, RANK), F32),
            pltpu.VMEM((RANK, RANK), F32),
            pltpu.VMEM((RANK, RANK), F32),
            pltpu.VMEM((nw, gc, RANK), F32),
            pltpu.VMEM((gc, RANK), F32),
            pltpu.VMEM((RANK, RANK), F32),
            pltpu.VMEM((4 * EDGE, 4 * RANK), BF16),
            pltpu.VMEM((EDGE * EDGE // 4, RANK), F32),
            pltpu.VMEM((EARLY * nb // 16, 4, EDGE * EDGE // 4, RANK), BF16),
            pltpu.VMEM((EDGE, RANK), F32),
            pltpu.VMEM((nb, EDGE, RANK), BF16),
            pltpu.VMEM((nb, EDGE, RANK), BF16),
            pltpu.VMEM((nw, fr, RANK), F32),
            pltpu.VMEM((nw, fr, RANK), F32),
            pltpu.VMEM((nb // 2, EDGE, RANK), F32),
            pltpu.VMEM((nb // 2, EDGE, RANK), F32),
            pltpu.VMEM((nb // 2, EDGE, RANK), F32),
            dma((5,)),
            dma((nb,)),
            dma((nb,)),
            dma((nb,)),
            dma((nb,)),
            dma((nb,)),
            dma((nb,)),
            dma((nb,)),
            dma((nb,)),
            dma((nb,)),
            dma((nb,)),
            dma((nb,)),
            dma((nw,)),
            dma((nw,)),
            dma((nw,)),
            dma((nw,)),
            dma((nb,)),
            dma((nb,)),
            dma((nw,)),
            dma((nw,)),
            dma((nb // 2,)),
            dma((nb // 2,)),
        ],
        compiler_params=pltpu.CompilerParams(
            collective_id=0, has_side_effects=True, vmem_limit_bytes=54 * 1024 * 1024
        ),
        name="cp_als",
    )(block_row, block_depth, live, blocks, factor_b, factor_c.reshape(-1, EDGE, RANK))


def solution(mesh):
    in_specs = (
        P(("blk", "wide"), None, None),
        P(("blk", "wide")),
        P(("blk", "wide")),
        P(("blk", "wide")),
        P("blk", None),
        P(),
    )
    out_specs = (P("wide", None), P(("blk", "wide"), None))
    body = functools.partial(per_device, mesh.shape["blk"], mesh.shape["wide"])
    return jax.shard_map(
        body, mesh=mesh, in_specs=in_specs, out_specs=out_specs, check_vma=False
    )
```

```python
import functools

import jax
import jax.numpy as jnp
from jax import lax
from jax.experimental import pallas as pl
from jax.experimental.pallas import tpu as pltpu
from jax.sharding import PartitionSpec as P

EDGE = 64
RANK = 256
ROW_BLOCKS = 4
RIDGE = 0.05
SCALE = 0.125 / EDGE
PANEL = 64
LAG = 3
EARLY = 7
F32 = jnp.float32
BF16 = jnp.bfloat16
MESH = pl.DeviceIdType.MESH
TN = (((0,), (0,)), ((), ()))


def split3(x):
    hi = x.astype(BF16)
    rest = x - hi.astype(F32)
    mid = rest.astype(BF16)
    low = (rest - mid.astype(F32)).astype(BF16)
    return hi, mid, low


def small_inverse(cols):
    sub = lax.broadcasted_iota(jnp.int32, (8, 128), 0)
    for k in range(0, 8, 2):
        row0 = [jnp.broadcast_to(c[k : k + 1, :], (8, 128)) for c in cols]
        row1 = [jnp.broadcast_to(c[k + 1 : k + 2, :], (8, 128)) for c in cols]
        p, q, r, s = row0[k], row0[k + 1], row1[k], row1[k + 1]
        inv = 1.0 / (p * s - q * r)
        col0, col1 = cols[k], cols[k + 1]
        new = []
        for j in range(8):
            if j == k:
                up, low = s * inv, -(r * inv)
            elif j == k + 1:
                up, low = -(q * inv), p * inv
            else:
                up = (s * row0[j] - q * row1[j]) * inv
                low = (p * row1[j] - r * row0[j]) * inv
            drop = col0 * up + col1 * low
            rest = -drop if j in (k, k + 1) else cols[j] - drop
            new.append(jnp.where(sub == k, up, jnp.where(sub == k + 1, low, rest)))
        cols = new
    return cols


def tree_sum(terms):
    while len(terms) > 1:
        terms = [terms[i] + terms[i + 1] for i in range(0, len(terms), 2)]
    return terms[0]


def panel_eliminate(groups):
    lane = lax.broadcasted_iota(jnp.int32, (8, RANK), 1)
    bits = [(lane & (1 << i)) != 0 for i in range(3)]
    count = len(groups)
    for s in range(count):
        base = 8 * s
        cols = [
            jnp.broadcast_to(groups[s][:, base + j : base + j + 1], (8, 128)) for j in range(8)
        ]
        others = {
            g: [jnp.broadcast_to(groups[g][:, base + j : base + j + 1], (8, RANK)) for j in range(8)]
            for g in range(count)
            if g != s
        }
        inv = [jnp.concatenate([c, c], axis=1) for c in small_inverse(cols)]
        placed = inv
        for bit in bits:
            placed = [
                jnp.where(bit, placed[i + 1], placed[i]) for i in range(0, len(placed), 2)
            ]
        inside = (lane >= base) & (lane < base + 8)
        rows = jnp.where(
            inside, placed[0], tree_sum([inv[j] * groups[s][j : j + 1, :] for j in range(8)])
        )
        spread = [jnp.broadcast_to(rows[j : j + 1, :], (8, RANK)) for j in range(8)]
        groups = [
            rows
            if g == s
            else jnp.where(inside, 0.0, groups[g])
            - tree_sum([others[g][j] * spread[j] for j in range(8)])
            for g in range(count)
        ]
    return groups


def invert_steps(mat, first, last):
    lane = lax.broadcasted_iota(jnp.int32, (1, RANK), 1)

    def step(p, carry):
        r0 = pl.multiple_of(p * PANEL, PANEL)
        panel = mat[pl.ds(r0, PANEL), :]
        rolled = pltpu.roll(panel, lax.rem(RANK - r0, RANK), 1)
        groups = panel_eliminate([rolled[8 * g : 8 * g + 8, :] for g in range(PANEL // 8)])
        rows = pltpu.roll(jnp.concatenate(groups, axis=0), r0, 1)
        before = lane < r0
        inside = (lane >= r0) & (lane < r0 + PANEL)
        sign = jnp.where(before, -1.0, jnp.where(inside, 0.0, 1.0))
        qh, qm, ql = split3(panel * sign)
        wh, wm, wl = split3(rows)
        left = jnp.concatenate([qh, qh, qh, qm, qm, ql], axis=0)
        right = jnp.concatenate([wh, wm, wl, wh, wm, wh], axis=0)
        for half in range(2):
            cut = pl.ds(half * 128, 128)
            update = lax.dot_general(
                left[:, half * 128 : half * 128 + 128], right, TN, preferred_element_type=F32
            )
            mat[cut, :] = jnp.where(inside, 0.0, mat[cut, :]) - update
        mat[pl.ds(r0, PANEL), :] = rows
        return carry

    lax.fori_loop(first, last, step, 0)


def kernel(
    nb,
    nw,
    total_rows,
    block_row_in,
    block_depth_in,
    live_in,
    blocks,
    fb_in,
    fc_in,
    out_a,
    out_b,
    block_row,
    block_depth,
    live,
    fb,
    fc,
    x,
    bg,
    acc,
    ra,
    ca,
    fa,
    gram_c,
    mat_a,
    mat_b,
    gl,
    gr,
    gs,
    gfull,
    bd,
    y,
    yc,
    tf,
    tsend,
    trecv,
    us,
    ur,
    cs,
    cr,
    tm,
    in_sem,
    x_sem,
    bz_s,
    bz_r,
    bx_s,
    bx_r,
    bc_s,
    bc_r,
    ra_s,
    ra_r,
    ca_s,
    ca_r,
    g1_s,
    g1_r,
    g2_s,
    g2_r,
    t_s,
    t_r,
    u_s,
    u_r,
    p_s,
    p_r,
):
    b = lax.axis_index("blk")
    w = lax.axis_index("wide")
    line = nb // 2
    half = EDGE // 2
    early = EARLY * nb // 16
    rc = ROW_BLOCKS * EDGE // nb
    gc = RANK // nw
    fr = EDGE // nw
    side = b // line
    place = lax.rem(b, line)
    core = lax.rem(w, 2)
    mate = w + 1 - 2 * core
    flip = w + 2 - 4 * lax.rem(w // 2, 2)
    across = (1 - side) * line + place

    def panel(t):
        k = lax.rem(t, line)
        odd = lax.rem(k, 2)
        d = odd * ((k + 1) // 2) + (1 - odd) * lax.rem(line - k // 2, line)
        return lax.rem(side + t // line, 2) * line + lax.rem(place + d, line)

    def slot_of(t):
        pairs = line // 2
        u = t // 2
        k = lax.rem(u, pairs)
        pair = lax.rem(place // 2 + pairs - 1 - k, pairs)
        far = 1 - u // pairs
        which = lax.rem(t, 2) * core + (1 - lax.rem(t, 2)) * (1 - core)
        return lax.rem(side + far, 2) * line + pair * 2 + which

    barrier = pltpu.get_barrier_semaphore()

    def signal(i, j):
        pl.semaphore_signal(barrier, inc=1, device_id=(i, j), device_id_type=MESH)

    def greet_blk(d, carry):
        signal(lax.rem(b + d, nb), w)
        return carry

    def greet_wide(d, carry):
        signal(b, lax.rem(w + d, nw))
        return carry

    lax.fori_loop(1, nb, greet_blk, 0)
    lax.fori_loop(1, nw, greet_wide, 0)
    signal(across, flip)

    small = [
        pltpu.make_async_copy(src, dst, in_sem.at[i])
        for i, (src, dst) in enumerate(
            [
                (fb_in, fb),
                (fc_in, fc),
                (block_row_in, block_row),
                (block_depth_in, block_depth),
                (live_in, live),
            ]
        )
    ]
    for copy in small:
        copy.start()

    def load_x(s):
        return pltpu.make_async_copy(blocks.at[s], x.at[s], x_sem.at[s])

    def start_x(t, carry):
        load_x(panel(t)).start()
        return carry

    lax.fori_loop(0, nb, start_x, 0)
    for copy in small:
        copy.wait()
    bg[b] = fb[...]
    acc[...] = jnp.zeros_like(acc)
    bd[...] = jnp.zeros_like(bd)
    pl.semaphore_wait(barrier, nb - 1 + nw - 1 + 1)

    rows_mine = pl.ds(pl.multiple_of(core * half, half), half)
    rows_mate = pl.ds(pl.multiple_of((1 - core) * half, half), half)

    def copy_bz(to, p):
        return pltpu.make_async_remote_copy(
            src_ref=fb.at[rows_mine, :],
            dst_ref=bg.at[p, rows_mine, :],
            send_sem=bz_s.at[to],
            recv_sem=bz_r.at[p],
            device_id=(to, w),
            device_id_type=MESH,
        )

    def copy_bx(p):
        return pltpu.make_async_remote_copy(
            src_ref=bg.at[p, rows_mine, :],
            dst_ref=bg.at[p, rows_mine, :],
            send_sem=bx_s.at[p],
            recv_sem=bx_r.at[p],
            device_id=(across, flip),
            device_id_type=MESH,
        )

    def copy_bc(p, rows):
        return pltpu.make_async_remote_copy(
            src_ref=bg.at[p, rows, :],
            dst_ref=bg.at[p, rows, :],
            send_sem=bc_s.at[p],
            recv_sem=bc_r.at[p],
            device_id=(b, mate),
            device_id_type=MESH,
        )

    def copy_own_x():
        return pltpu.make_async_remote_copy(
            src_ref=fb.at[rows_mine, :],
            dst_ref=bg.at[b, rows_mine, :],
            send_sem=bx_s.at[b],
            recv_sem=bx_r.at[b],
            device_id=(across, flip),
            device_id_type=MESH,
        )

    def start_bz(t, carry):
        copy_bz(panel(t), b).start()
        return carry

    lax.fori_loop(1, 2, start_bz, 0)
    copy_own_x().start()
    lax.fori_loop(2, line, start_bz, 0)

    def share(g, r):
        row = block_row[g].astype(F32)
        return jnp.maximum(0.0, 1.0 - jnp.abs(row - r)) * live[g].astype(F32)

    def first_slot(g):
        crows = fc[block_depth[g]]
        term = jnp.zeros((EDGE, RANK), F32)
        for jg in range(EDGE // 4):
            brows = bg[g, pl.ds(jg * 4 // 16 * 16, 16), :]
            off = jg * 4 % 16
            pair = jnp.concatenate(
                [brows[off + q : off + q + 1, :] * crows for q in range(4)], axis=0
            )
            term += jnp.dot(
                x[g, :, pl.ds(jg * 256, 256)], pair, preferred_element_type=F32
            )
        for r in range(ROW_BLOCKS):
            cut = pl.ds(r * EDGE, EDGE)
            acc[cut, :] = acc[cut, :] + term * share(g, r)

    def first_loop(t, carry):
        p = panel(t)

        @pl.when((t > 0) & (t < line))
        def _():
            copy_bz(p, p).wait_recv()
            copy_bx(p).start()
            copy_bc(p, rows_mine).start()

        @pl.when((t >= line) & (t < nb))
        def _():
            copy_bx(p).wait_recv()
            copy_bc(p, rows_mine).start()

        @pl.when(t > LAG)
        def _():
            copy_bc(panel(t - LAG), rows_mate).wait_recv()

        @pl.when(t >= LAG)
        def _():
            g = panel(t - LAG)
            load_x(g).wait()
            first_slot(g)

        return carry

    cfull = fc[...].reshape(fc.shape[0] * EDGE, RANK)
    gram_c[...] = lax.dot_general(cfull, cfull, TN, preferred_element_type=F32) * (
        1.0 / cfull.shape[0]
    )
    lax.fori_loop(1, nb + LAG, first_loop, 0)

    def copy_ra(peer, slot):
        return pltpu.make_async_remote_copy(
            src_ref=acc.at[pl.ds(pl.multiple_of(peer * rc, rc), rc), :],
            dst_ref=ra.at[slot],
            send_sem=ra_s.at[peer],
            recv_sem=ra_r.at[slot],
            device_id=(peer, w),
            device_id_type=MESH,
        )

    def start_ra(t, carry):
        copy_ra(panel(nb - t), b).start()
        return carry

    lax.fori_loop(1, nb, start_ra, 0)

    bfull = bg[...].reshape(nb * EDGE, RANK)
    gram_b = lax.dot_general(bfull, bfull, TN, preferred_element_type=F32) * (1.0 / (nb * EDGE))
    eye = lax.broadcasted_iota(jnp.int32, (RANK, RANK), 0) == lax.broadcasted_iota(
        jnp.int32, (RANK, RANK), 1
    )
    mat_a[...] = gram_c[...] * gram_b + jnp.where(eye, RIDGE, 0.0)
    invert_steps(mat_a, 0, RANK // PANEL)

    own_rows = pl.ds(pl.multiple_of(b * rc, rc), rc)

    def sum_ra(t, total):
        s = panel(t)
        copy_ra(s, s).wait_recv()
        return total + ra[s]

    rows_a = lax.fori_loop(1, nb, sum_ra, acc[own_rows, :])
    solved = jnp.dot(
        rows_a, mat_a[...], preferred_element_type=F32, precision=lax.Precision.HIGHEST
    )
    ca[...] = (solved * SCALE).astype(BF16)

    def copy_ca(peer, s):
        return pltpu.make_async_remote_copy(
            src_ref=ca,
            dst_ref=fa.at[pl.ds(pl.multiple_of(s * rc, rc), rc), :],
            send_sem=ca_s.at[peer],
            recv_sem=ca_r.at[s],
            device_id=(peer, w),
            device_id_type=MESH,
        )

    def start_ca(t, carry):
        copy_ca(panel(nb - t), b).start()
        return carry

    def wait_ca(t, carry):
        s = panel(t)
        copy_ca(s, s).wait_recv()
        return carry

    lax.fori_loop(1, nb, start_ca, 0)
    fa[own_rows, :] = ca[...]

    def depth_operands(g):
        crows = fc[block_depth[g]]
        for q in range(4):
            bd[pl.ds(q * EDGE, EDGE), pl.ds(q * RANK, RANK)] = crows
        return jnp.concatenate(
            [x[g, :, pl.ds(jg * 256, 256)] for jg in range(EDGE // 4)], axis=0
        )

    def early_loop(t, carry):
        lhs = depth_operands(slot_of(t))
        for q in range(4):
            yc[t, q] = jnp.dot(
                lhs, bd[:, pl.ds(q * RANK, RANK)], preferred_element_type=F32
            ).astype(BF16)
        return carry

    lax.fori_loop(0, early, early_loop, 0)
    lax.fori_loop(1, nb, wait_ca, 0)

    gl[...] = lax.dot_general(fa[...], fa[...], TN, preferred_element_type=F32)

    def gram_rows(v):
        return pl.ds(pl.multiple_of(v * gc, gc), gc)

    def copy_g1(peer, slot):
        return pltpu.make_async_remote_copy(
            src_ref=gl.at[gram_rows(peer), :],
            dst_ref=gr.at[slot],
            send_sem=g1_s.at[peer],
            recv_sem=g1_r.at[slot],
            device_id=(b, peer),
            device_id_type=MESH,
        )

    def start_g1(d, carry):
        copy_g1(lax.rem(w + d, nw), w).start()
        return carry

    lax.fori_loop(1, nw, start_g1, 0)
    out_a[...] = fa[...]

    def copy_t(peer, slot):
        return pltpu.make_async_remote_copy(
            src_ref=tsend.at[peer],
            dst_ref=trecv.at[slot],
            send_sem=t_s.at[peer],
            recv_sem=t_r.at[slot],
            device_id=(peer, w),
            device_id_type=MESH,
        )

    def weighted_rows(g):
        arows = jnp.zeros((EDGE, RANK), F32)
        for r in range(ROW_BLOCKS):
            arows += fa[pl.ds(r * EDGE, EDGE), :].astype(F32) * share(g, r)
        return arows

    def second_slot(g):
        arows = weighted_rows(g)
        lhs = depth_operands(g)
        for q in range(4):
            y[...] = jnp.dot(lhs, bd[:, pl.ds(q * RANK, RANK)], preferred_element_type=F32)
            for jg in range(EDGE // 4):
                prod = y[pl.ds(jg * EDGE, EDGE), :] * arows
                tf[pl.ds(jg * 4 + q, 1), :] = jnp.sum(prod, axis=0, keepdims=True)

    def second_early(t, g):
        arows = weighted_rows(g)
        for q in range(4):
            for jg in range(EDGE // 4):
                prod = yc[t, q, pl.ds(jg * EDGE, EDGE), :].astype(F32) * arows
                tf[pl.ds(jg * 4 + q, 1), :] = jnp.sum(prod, axis=0, keepdims=True)

    def copy_g2(peer, s):
        return pltpu.make_async_remote_copy(
            src_ref=gs,
            dst_ref=gfull.at[gram_rows(s), :],
            send_sem=g2_s.at[peer],
            recv_sem=g2_r.at[s],
            device_id=(b, peer),
            device_id_type=MESH,
        )

    def copy_pair(u):
        return pltpu.make_async_remote_copy(
            src_ref=cs.at[u],
            dst_ref=cr.at[u],
            send_sem=p_s.at[u],
            recv_sem=p_r.at[u],
            device_id=(b, mate),
            device_id_type=MESH,
        )

    def pass_on(u):
        copy_pair(u).wait_recv()
        g = slot_of(2 * u + 1)
        tsend[g] = (tm[u] + cr[u]).astype(BF16)

        @pl.when(g != b)
        def _():
            copy_t(g, b).start()

    def after_slot(t):
        u = t // 2

        @pl.when(lax.rem(t, 2) == 0)
        def _():
            cs[u] = tf[...]
            copy_pair(u).start()

        @pl.when(lax.rem(t, 2) == 1)
        def _():
            tm[u] = tf[...]

            @pl.when(u > 0)
            def _():
                pass_on(u - 1)

    def second_first(t, carry):
        second_early(t, slot_of(t))
        after_slot(t)
        return carry

    def second_loop(t, carry):
        @pl.when(t == nb // 2)
        def _():
            def sum_g1(d, total):
                s = lax.rem(w + d, nw)
                copy_g1(s, s).wait_recv()
                return total + gr[s]

            def start_g2(d, carry):
                copy_g2(lax.rem(w + d, nw), w).start()
                return carry

            gs[...] = lax.fori_loop(1, nw, sum_g1, gl[gram_rows(w), :])
            lax.fori_loop(1, nw, start_g2, 0)

        second_slot(slot_of(t))
        after_slot(t)
        return carry

    lax.fori_loop(0, early, second_first, 0)
    lax.fori_loop(early, nb, second_loop, 0)
    pass_on(nb // 2 - 1)
    gfull[gram_rows(w), :] = gs[...]

    def wait_g2(d, carry):
        s = lax.rem(w + d, nw)
        copy_g2(s, s).wait_recv()
        return carry

    lax.fori_loop(1, nw, wait_g2, 0)
    mat_b[...] = gram_c[...] * (gfull[...] * (1.0 / total_rows)) + jnp.where(eye, RIDGE, 0.0)
    invert_steps(mat_b, 0, RANK // PANEL // 2)

    holds = lax.rem(b, 2) == core

    @pl.when(holds)
    def _():
        def sum_t(t, total):
            s = panel(nb - t)
            copy_t(s, s).wait_recv()
            return total + trecv[s].astype(F32)

        own_t = tm[nb // 2 - 1] + cr[nb // 2 - 1]
        rows_t = lax.fori_loop(1, nb, sum_t, own_t)
        for v in range(nw):
            us[v] = rows_t[v * fr : (v + 1) * fr, :]

    def copy_u(peer, slot):
        return pltpu.make_async_remote_copy(
            src_ref=us.at[peer],
            dst_ref=ur.at[slot],
            send_sem=u_s.at[peer],
            recv_sem=u_r.at[slot],
            device_id=(b, peer),
            device_id_type=MESH,
        )

    def start_u(d, carry):
        copy_u(lax.rem(w + d, nw), w).start()
        return carry

    @pl.when(holds)
    def _():
        lax.fori_loop(1, nw, start_u, 0)

    invert_steps(mat_b, RANK // PANEL // 2, RANK // PANEL)

    @pl.when(holds)
    def _():
        ur[w] = us[w]

    def sum_u(i, total):
        s = 2 * i + lax.rem(b, 2)

        @pl.when(s != w)
        def _():
            copy_u(s, s).wait_recv()

        return total + ur[s]

    rows_b = lax.fori_loop(0, nw // 2, sum_u, jnp.zeros((fr, RANK), F32))
    pad = jnp.concatenate([rows_b] * max(1, 8 // fr), axis=0)
    new_b = jnp.dot(pad, mat_b[...], preferred_element_type=F32, precision=lax.Precision.HIGHEST)
    out_b[...] = (new_b[:fr, :] * SCALE).astype(BF16)

    def drain_line(t, carry):
        p = panel(t)
        copy_bz(p, b).wait_send()
        copy_bx(p).wait_send()
        return carry

    def drain_blk(t, carry):
        p = panel(t)
        copy_bc(p, rows_mine).wait_send()
        copy_ra(p, b).wait_send()
        copy_ca(p, b).wait_send()

        @pl.when(lax.rem(p, 2) == core)
        def _():
            copy_t(p, b).wait_send()

        return carry

    def drain_wide(d, carry):
        peer = lax.rem(w + d, nw)
        copy_g1(peer, w).wait_send()
        copy_g2(peer, w).wait_send()

        @pl.when(holds)
        def _():
            copy_u(peer, w).wait_send()

        return carry

    def drain_pair(u, carry):
        copy_pair(u).wait_send()
        return carry

    copy_own_x().wait_send()
    lax.fori_loop(1, line, drain_line, 0)
    lax.fori_loop(1, nb, drain_blk, 0)
    lax.fori_loop(1, nw, drain_wide, 0)
    lax.fori_loop(0, nb // 2, drain_pair, 0)


def per_device(nb, nw, blocks, block_row, block_depth, live, factor_b, factor_c):
    rows_a = ROW_BLOCKS * EDGE
    rc, gc, fr = rows_a // nb, RANK // nw, EDGE // nw
    vm = pl.BlockSpec(memory_space=pltpu.VMEM)
    depth = factor_c.shape[0] // EDGE
    dma = pltpu.SemaphoreType.DMA
    return pl.pallas_call(
        functools.partial(kernel, nb, nw, nw * rows_a),
        out_shape=(
            jax.ShapeDtypeStruct((rows_a, RANK), BF16),
            jax.ShapeDtypeStruct((fr, RANK), BF16),
        ),
        in_specs=[pl.BlockSpec(memory_space=pltpu.HBM)] * 6,
        out_specs=(vm, vm),
        scratch_shapes=[
            pltpu.SMEM((nb,), jnp.int32),
            pltpu.SMEM((nb,), jnp.int32),
            pltpu.SMEM((nb,), jnp.int32),
            pltpu.VMEM((EDGE, RANK), BF16),
            pltpu.VMEM((depth, EDGE, RANK), BF16),
            pltpu.VMEM((nb, EDGE, EDGE * EDGE), BF16),
            pltpu.VMEM((nb, EDGE, RANK), BF16),
            pltpu.VMEM((rows_a, RANK), F32),
            pltpu.VMEM((nb, rc, RANK), F32),
            pltpu.VMEM((rc, RANK), BF16),
            pltpu.VMEM((rows_a, RANK), BF16),
            pltpu.VMEM((RANK, RANK), F32),
            pltpu.VMEM((RANK, RANK), F32),
            pltpu.VMEM((RANK, RANK), F32),
            pltpu.VMEM((RANK, RANK), F32),
            pltpu.VMEM((nw, gc, RANK), F32),
            pltpu.VMEM((gc, RANK), F32),
            pltpu.VMEM((RANK, RANK), F32),
            pltpu.VMEM((4 * EDGE, 4 * RANK), BF16),
            pltpu.VMEM((EDGE * EDGE // 4, RANK), F32),
            pltpu.VMEM((EARLY * nb // 16, 4, EDGE * EDGE // 4, RANK), BF16),
            pltpu.VMEM((EDGE, RANK), F32),
            pltpu.VMEM((nb, EDGE, RANK), BF16),
            pltpu.VMEM((nb, EDGE, RANK), BF16),
            pltpu.VMEM((nw, fr, RANK), F32),
            pltpu.VMEM((nw, fr, RANK), F32),
            pltpu.VMEM((nb // 2, EDGE, RANK), F32),
            pltpu.VMEM((nb // 2, EDGE, RANK), F32),
            pltpu.VMEM((nb // 2, EDGE, RANK), F32),
            dma((5,)),
            dma((nb,)),
            dma((nb,)),
            dma((nb,)),
            dma((nb,)),
            dma((nb,)),
            dma((nb,)),
            dma((nb,)),
            dma((nb,)),
            dma((nb,)),
            dma((nb,)),
            dma((nb,)),
            dma((nw,)),
            dma((nw,)),
            dma((nw,)),
            dma((nw,)),
            dma((nb,)),
            dma((nb,)),
            dma((nw,)),
            dma((nw,)),
            dma((nb // 2,)),
            dma((nb // 2,)),
        ],
        compiler_params=pltpu.CompilerParams(
            collective_id=0, has_side_effects=True, vmem_limit_bytes=54 * 1024 * 1024
        ),
        name="cp_als",
    )(block_row, block_depth, live, blocks, factor_b, factor_c.reshape(-1, EDGE, RANK))


def solution(mesh):
    in_specs = (
        P(("blk", "wide"), None, None),
        P(("blk", "wide")),
        P(("blk", "wide")),
        P(("blk", "wide")),
        P("blk", None),
        P(),
    )
    out_specs = (P("wide", None), P(("blk", "wide"), None))
    body = functools.partial(per_device, mesh.shape["blk"], mesh.shape["wide"])
    return jax.shard_map(
        body, mesh=mesh, in_specs=in_specs, out_specs=out_specs, check_vma=False
    )
```
